256 devices in a mesh: patch: 128 (over y, z, x), vec: 2 (over core).
Axes of the slice: x: 4, y: 4, z: 8, core: 2. Of those that a mesh axis runs over, the one named last changes fastest.
Arguments:
- vectors: float32 [65536, 512], P('patch', 'vec'), may hold values from -6 to 6
- blocks: bfloat16 [8192, 256, 256], P('patch'), may hold values from -0.075 to 0.075, as said below
- block_row: int32 [8192], P('patch'), may hold values from 0 to 255, as said below
- block_col: int32 [8192], P('patch'), may hold values from 0 to 255, as said below
- block_count: int32 [128], P('patch'), may hold values from 0 to 58, as said below
Outputs:
- subspace: float32 [65536, 512], P('patch', 'vec')
- residual: float32 [65536, 512], P('patch', 'vec')
The draws below stay inside these ranges and needn't reach their ends.
Inputs may be any that keep to these rules, and one draw needn't show every extreme that they name: `block_row`: device p owns entries p * 64 to (p + 1) * 64 - 1. Its used slots come first and hold tiles of block rows 4 * (p // 2) to 4 * (p // 2) + 3 whose block column is at most the row and at least 4 * (p // 2) - 12; both devices of a pair p // 2 share these rows, tiles grouped by 4 x 4 patches each on one device. Every lower tile of the pattern stands in exactly one used slot, every diagonal tile is present, and unused slots name block row and column 4 * (p // 2). `block_col`: the block column of the tile in the same slot, as described for block_row. `block_count`: at most 58 used slots on a device, reached by some device in every draw; the loads are uneven. `blocks`: entries of unused slots are never read.
All inputs are finite; a program needn't handle non-finite values.
Results may differ from the reference program's by a relative error of at most 0.0038.
Values may be sent and summed in bfloat16 or wider, within the bound.
A program may use at most 128 MiB of HBM per device.

```python
import jax
import jax.numpy as jnp
from jax import lax

BS = 256
K = 512
BLK_DEV = 64
STEPS = 2
NH = 65536


def slot_layout(key):
    key = jax.random.fold_in(key, 7919)
    pair_total = NH // (4 * BS)
    key_owner, key_keep, key_star = jax.random.split(key, 3)
    owners = jax.random.randint(key_owner, (pair_total, 4), 0, 2)
    keeps = jax.random.randint(key_keep, (pair_total, 4, 4, 4), 0, 4) > 0
    starred = jax.random.randint(key_star, (), 3, pair_total)
    is_star = jnp.arange(pair_total) == starred
    owners = jnp.where(is_star[:, None], 0, owners)
    keeps = keeps | is_star[:, None, None, None]
    pair_ids = jnp.arange(pair_total)[:, None, None, None]
    diag_off = jnp.arange(4)[None, :, None, None]
    sub_row = jnp.arange(4)[None, None, :, None]
    sub_col = jnp.arange(4)[None, None, None, :]
    shape_full = (pair_total, 4, 4, 4)
    row_ids = jnp.broadcast_to(4 * pair_ids + sub_row, shape_full)
    col_ids = jnp.broadcast_to(4 * (pair_ids - diag_off) + sub_col, shape_full)
    valid = (pair_ids - diag_off >= 0) & ((diag_off > 0) | (sub_row >= sub_col))
    present = valid & (keeps | (diag_off == 0) & (sub_row == sub_col))
    owner_full = owners[:, :, None, None]
    take_low = present & (owner_full == 0)
    take_high = present & (owner_full == 1)
    taken = jnp.stack([take_low, take_high], axis=1).reshape(pair_total * 2, 64)
    rows_flat = jnp.broadcast_to(row_ids.reshape(pair_total, 1, 64), (pair_total, 2, 64)).reshape(pair_total * 2, 64)
    cols_flat = jnp.broadcast_to(col_ids.reshape(pair_total, 1, 64), (pair_total, 2, 64)).reshape(pair_total * 2, 64)
    position = jnp.arange(64)[None, :]
    sort_key = jnp.where(taken, position, 64 + position)
    order = jnp.argsort(sort_key, axis=1)
    taken_sorted = jnp.take_along_axis(taken, order, axis=1)
    rows_sorted = jnp.take_along_axis(rows_flat, order, axis=1)
    cols_sorted = jnp.take_along_axis(cols_flat, order, axis=1)
    home = (4 * (jnp.arange(pair_total * 2) // 2))[:, None]
    rows_final = jnp.where(taken_sorted, rows_sorted, home).reshape(-1).astype(jnp.int32)
    cols_final = jnp.where(taken_sorted, cols_sorted, home).reshape(-1).astype(jnp.int32)
    counts = jnp.sum(taken.astype(jnp.int32), axis=1).astype(jnp.int32)
    return (rows_final, cols_final, counts)


def draw_block_row(key, part):
    return slot_layout(key)[0]


def draw_block_col(key, part):
    return slot_layout(key)[1]


def draw_block_count(key, part):
    return slot_layout(key)[2]


def draw_blocks(key, part):
    key = jax.random.fold_in(key, 4241)
    slot_total = NH // (2 * BS) * BLK_DEV
    spread = 1.0 / (5.0 * BS ** 0.5)
    limit = 0.99 * 6.0 * spread
    shared = 0.9 / BS
    noise = jnp.clip(jax.random.normal(key, (slot_total, BS, BS), jnp.float32), -5.5, 5.5) * spread
    values = jnp.clip(noise + shared, -limit, limit)
    return values.astype(jnp.bfloat16)


def level_of(own_key, shape, cuts, smallest, largest):
    loudness, own = 1.0, jax.random.fold_in(own_key, 6)
    for axis_at, shards_of in cuts:
        draws = jnp.exp(jax.random.uniform(jax.random.fold_in(own, axis_at), (shards_of,), jnp.float32, smallest / len(cuts), largest / len(cuts)))
        loudness = loudness * jnp.repeat(draws, shape[axis_at] // shards_of).reshape([-1 if axis == axis_at else 1 for axis in range(len(shape))])
    return loudness


def centred(own_key, extent, scale, most, pieces=(), kind=jnp.bfloat16):
    factor_of = level_of(own_key, extent, pieces, -0.22, 0.18) if pieces else 1.0
    values = jax.random.normal(own_key, extent, jnp.float32) * scale * factor_of
    return jnp.minimum(jnp.maximum(values, -most), most).astype(kind)


def setup_inputs(seed: int = 0) -> dict:
    seeds = jax.random.split(jax.random.key(seed), 6)
    return {
        "vectors": centred(seeds[0], (NH, K), 1.0, 6.0, ((0, 128), (1, 2)), jnp.float32),
        "blocks": draw_blocks(jax.random.fold_in(seeds[5], 71), 0),
        "block_row": draw_block_row(jax.random.fold_in(seeds[5], 71), 0),
        "block_col": draw_block_col(jax.random.fold_in(seeds[5], 71), 0),
        "block_count": draw_block_count(jax.random.fold_in(seeds[5], 71), 0),
    }


step_rate = 0.25
exact_mode = lax.Precision.HIGHEST

def hessian_apply(rounded, blocks, block_row, block_col, block_count):
    nblock = NH // BS
    ndevice = NH // (2 * BS)
    block_tiles = rounded.astype(jnp.float32).reshape(nblock, BS, K)

    def per_device(totals, device):
        slot_start = device * BLK_DEV
        chosen = lax.dynamic_slice_in_dim(blocks, slot_start, BLK_DEV, 0).astype(jnp.float32)
        row_ids = lax.dynamic_slice_in_dim(block_row, slot_start, BLK_DEV, 0)
        col_ids = lax.dynamic_slice_in_dim(block_col, slot_start, BLK_DEV, 0)
        used_slots = lax.dynamic_index_in_dim(block_count, device, 0, keepdims=False)
        alive_mask = (jnp.arange(BLK_DEV, dtype=jnp.int32) < used_slots).astype(jnp.float32)
        weight = (jnp.where(row_ids == col_ids, 0.5, 1.0).astype(jnp.float32) * alive_mask)[:, None, None]
        direct = jnp.einsum('sab,sbk->sak', chosen, block_tiles[col_ids], precision=exact_mode) * weight
        mirror = jnp.einsum('sba,sbk->sak', chosen, block_tiles[row_ids], precision=exact_mode) * weight
        totals = totals.at[row_ids].add(direct).at[col_ids].add(mirror)
        return (totals, None)
    start_total = jnp.zeros((nblock, BS, K), jnp.float32)
    totals, _unused = lax.scan(per_device, start_total, jnp.arange(ndevice, dtype=jnp.int32))
    return totals.reshape(NH, K)

def reference(vectors, blocks, block_row, block_col, block_count):
    current = vectors
    residual = vectors
    for iteration in range(STEPS):
        rounded = current.astype(jnp.bfloat16)
        applied = hessian_apply(rounded, blocks, block_row, block_col, block_count)
        rayleigh = jnp.dot(current.T.astype(jnp.float32), applied.astype(jnp.float32), precision=exact_mode, preferred_element_type=jnp.float32) / NH
        residual = applied - jnp.dot(current.astype(jnp.float32), rayleigh.astype(jnp.float32), precision=exact_mode, preferred_element_type=jnp.float32)
        update = current - step_rate * residual
        gram_matrix = jnp.dot(update.T.astype(jnp.float32), update.astype(jnp.float32), precision=exact_mode, preferred_element_type=jnp.float32) / NH
        factor = jnp.linalg.cholesky(gram_matrix)
        current = lax.linalg.triangular_solve(factor, update, left_side=False, lower=True, transpose_a=True)
    return (current, residual)
```

```python
import jax
import jax.numpy as jnp
from jax import lax
from jax.sharding import PartitionSpec as P

STEPS = 2


step_rate = 0.25
exact_mode = lax.Precision.HIGHEST


def shifted(block, axis, distance):
    devices = range(lax.axis_size(axis))
    route = [(i - distance, i) for i in devices if i - distance in devices]
    return lax.ppermute(block, axis, route)


def summed_over_patch(block):
    size = lax.axis_size("patch")
    me = lax.axis_index("patch")
    bits = [b for b in (0, 2, 5, 1, 3, 6, 4) if (1 << b) < size]
    held = block
    for b in bits:
        half = held.shape[0] // 2
        side = (me >> b) & 1
        keep = lax.dynamic_slice_in_dim(held, side * half, half, 0)
        send = lax.dynamic_slice_in_dim(held, (1 - side) * half, half, 0)
        route = [(i, i ^ (1 << b)) for i in range(size)]
        held = keep + lax.ppermute(send, "patch", route)
    for b in reversed(bits):
        side = (me >> b) & 1
        route = [(i, i ^ (1 << b)) for i in range(size)]
        other = lax.ppermute(held, "patch", route)
        both = jnp.stack([held, other, held])
        held = lax.dynamic_slice_in_dim(both, side, 2, 0).reshape(-1, *held.shape[1:])
    return held


def accumulate(window_x, totals, block_tiles, row_ids, col_ids, used_slots, window_start):
    group_total = (used_slots + 7) // 8

    def one_turn(group_index, partial_value):
        first_slot = group_index * 8
        chosen = lax.dynamic_slice_in_dim(block_tiles, first_slot, 8, 0)
        rows_here = lax.dynamic_slice_in_dim(row_ids, first_slot, 8, 0) - window_start
        cols_here = lax.dynamic_slice_in_dim(col_ids, first_slot, 8, 0) - window_start
        alive_mask = (first_slot + jnp.arange(8, dtype=jnp.int32) < used_slots).astype(jnp.float32)
        weight = (jnp.where(rows_here == cols_here, 0.5, 1.0).astype(jnp.float32) * alive_mask)[
            :, None, None
        ]
        direct = (
            jnp.einsum(
                "sab,sbk->sak", chosen, window_x[cols_here], preferred_element_type=jnp.float32
            )
            * weight
        )
        mirror = (
            jnp.einsum(
                "sba,sbk->sak", chosen, window_x[rows_here], preferred_element_type=jnp.float32
            )
            * weight
        )
        return partial_value.at[rows_here].add(direct).at[cols_here].add(mirror)

    return lax.fori_loop(0, group_total, one_turn, totals)


def shards(vectors, blocks, block_row, block_col, block_count):
    dev_rows, col_width = vectors.shape
    tile_size = blocks.shape[1]
    total_rows = dev_rows * lax.axis_size("patch")
    position = lax.axis_index("patch")
    parity = position % 2
    window_start = 2 * (position - 6 - parity)
    column_start = lax.axis_index("vec") * col_width
    used_slots = block_count[0]
    current = vectors
    residual = vectors
    for iteration in range(STEPS):
        rounded = current.astype(jnp.bfloat16)
        pieces = {0: rounded}
        for offset in (7, 6, 5, 4, 3, 2, 1, -1):
            pieces[offset] = shifted(rounded, "patch", offset)
        lower_side = jnp.concatenate([pieces[6 - segment] for segment in range(8)], axis=0)
        upper_side = jnp.concatenate([pieces[7 - segment] for segment in range(8)], axis=0)
        window_x = jnp.where(parity == 0, lower_side, upper_side).reshape(16, tile_size, col_width)
        totals = jnp.zeros((16, tile_size, col_width), jnp.float32)
        totals = accumulate(
            window_x, totals, blocks, block_row, block_col, used_slots, window_start
        )
        segments = totals.reshape(8, dev_rows, col_width)
        zero_rows = jnp.zeros((dev_rows, col_width), jnp.float32)
        applied = jnp.where(parity == 0, segments[6], segments[7])
        for offset in (1, -1, -2, -3, -4, -5, -6, -7):
            lower_seg = segments[offset + 6] if 0 <= offset + 6 <= 7 else zero_rows
            upper_seg = segments[offset + 7] if 0 <= offset + 7 <= 7 else zero_rows
            outgoing = jnp.where(parity == 0, lower_seg, upper_seg)
            applied = applied + shifted(outgoing, "patch", offset)
        current_all = lax.all_gather(current, "vec", axis=1, tiled=True)
        rayleigh = summed_over_patch(
            jnp.dot(
                current_all.T, applied, precision=exact_mode, preferred_element_type=jnp.float32
            )
            / total_rows
        )
        residual = applied - jnp.dot(
            current_all, rayleigh, precision=exact_mode, preferred_element_type=jnp.float32
        )
        update = current - step_rate * residual
        update_all = lax.all_gather(update, "vec", axis=1, tiled=True)
        gram_matrix = summed_over_patch(
            jnp.dot(
                update_all.T, update_all, precision=exact_mode, preferred_element_type=jnp.float32
            )
            / total_rows
        )
        factor = jnp.linalg.cholesky(gram_matrix)
        solved = lax.linalg.triangular_solve(
            factor, update_all, left_side=False, lower=True, transpose_a=True
        )
        current = lax.dynamic_slice_in_dim(solved, column_start, col_width, 1)
    return (current, residual)


def solution(mesh):
    in_specs = (P("patch", "vec"), P("patch", None, None), P("patch"), P("patch"), P("patch"))
    out_specs = (P("patch", "vec"), P("patch", "vec"))
    return jax.shard_map(shards, mesh=mesh, in_specs=in_specs, out_specs=out_specs, check_vma=False)
```

```python
import jax
import jax.numpy as jnp
from jax import lax
from jax.experimental import pallas as pl
from jax.experimental.pallas import tpu as pltpu
from jax.sharding import PartitionSpec as P

STEPS = 2


step_rate = 0.25
exact_mode = lax.Precision.HIGHEST


def shifted(block, axis, distance):
    devices = range(lax.axis_size(axis))
    route = [(i - distance, i) for i in devices if i - distance in devices]
    return lax.ppermute(block, axis, route)


def summed_over_patch(block):
    size = lax.axis_size("patch")
    me = lax.axis_index("patch")
    bits = [b for b in (0, 2, 5, 1, 3, 6, 4) if (1 << b) < size]
    held = block
    for b in bits:
        half = held.shape[0] // 2
        side = (me >> b) & 1
        keep = lax.dynamic_slice_in_dim(held, side * half, half, 0)
        send = lax.dynamic_slice_in_dim(held, (1 - side) * half, half, 0)
        route = [(i, i ^ (1 << b)) for i in range(size)]
        held = keep + lax.ppermute(send, "patch", route)
    for b in reversed(bits):
        side = (me >> b) & 1
        route = [(i, i ^ (1 << b)) for i in range(size)]
        other = lax.ppermute(held, "patch", route)
        both = jnp.stack([held, other, held])
        held = lax.dynamic_slice_in_dim(both, side, 2, 0).reshape(-1, *held.shape[1:])
    return held


def tile_products(rows_ref, cols_ref, used_ref, tile_ref, x_ref, out_ref):
    slot = pl.program_id(0)

    @pl.when(slot == 0)
    def _():
        out_ref[...] = jnp.zeros_like(out_ref)

    @pl.when(slot < used_ref[0])
    def _():
        row = rows_ref[slot]
        col = cols_ref[slot]
        tile = tile_ref[0]
        weight = jnp.where(row == col, jnp.float32(0.5), jnp.float32(1.0))
        direct = jnp.dot(tile, x_ref[col], preferred_element_type=jnp.float32)
        out_ref[row] += direct * weight
        mirror = lax.dot_general(
            tile, x_ref[row], (((0,), (0,)), ((), ())), preferred_element_type=jnp.float32
        )
        out_ref[col] += mirror * weight


def hessian_window(window_x, blocks, rows_local, cols_local, used):
    slots, tile_size, _ = blocks.shape
    window_tiles, _, col_width = window_x.shape

    def tile_at(slot, rows, cols, used_ref):
        return (jnp.maximum(jnp.minimum(slot, used_ref[0] - 1), 0), 0, 0)

    def whole(slot, rows, cols, used_ref):
        return (0, 0, 0)

    grid_spec = pltpu.PrefetchScalarGridSpec(
        num_scalar_prefetch=3,
        grid=(slots,),
        in_specs=[
            pl.BlockSpec((1, tile_size, tile_size), tile_at),
            pl.BlockSpec((window_tiles, tile_size, col_width), whole),
        ],
        out_specs=pl.BlockSpec((window_tiles, tile_size, col_width), whole),
    )
    flops = 4 * slots * tile_size * tile_size * col_width
    return pl.pallas_call(
        tile_products,
        grid_spec=grid_spec,
        out_shape=jax.ShapeDtypeStruct((window_tiles, tile_size, col_width), jnp.float32),
        compiler_params=pltpu.CompilerParams(dimension_semantics=("arbitrary",)),
        cost_estimate=pl.CostEstimate(
            flops=flops,
            bytes_accessed=blocks.size * 2 + window_x.size * 2 + window_tiles * tile_size * col_width * 4,
            transcendentals=0,
        ),
    )(rows_local, cols_local, used, blocks, window_x)


def accumulate(window_x, totals, block_tiles, row_ids, col_ids, used_slots, window_start):
    group_total = (used_slots + 7) // 8

    def one_turn(group_index, partial_value):
        first_slot = group_index * 8
        chosen = lax.dynamic_slice_in_dim(block_tiles, first_slot, 8, 0)
        rows_here = lax.dynamic_slice_in_dim(row_ids, first_slot, 8, 0) - window_start
        cols_here = lax.dynamic_slice_in_dim(col_ids, first_slot, 8, 0) - window_start
        alive_mask = (first_slot + jnp.arange(8, dtype=jnp.int32) < used_slots).astype(jnp.float32)
        weight = (jnp.where(rows_here == cols_here, 0.5, 1.0).astype(jnp.float32) * alive_mask)[
            :, None, None
        ]
        direct = (
            jnp.einsum(
                "sab,sbk->sak", chosen, window_x[cols_here], preferred_element_type=jnp.float32
            )
            * weight
        )
        mirror = (
            jnp.einsum(
                "sba,sbk->sak", chosen, window_x[rows_here], preferred_element_type=jnp.float32
            )
            * weight
        )
        return partial_value.at[rows_here].add(direct).at[cols_here].add(mirror)

    return lax.fori_loop(0, group_total, one_turn, totals)


def shards(vectors, blocks, block_row, block_col, block_count):
    dev_rows, col_width = vectors.shape
    tile_size = blocks.shape[1]
    total_rows = dev_rows * lax.axis_size("patch")
    position = lax.axis_index("patch")
    parity = position % 2
    window_start = 2 * (position - 6 - parity)
    column_start = lax.axis_index("vec") * col_width
    used_slots = block_count[0]
    current = vectors
    residual = vectors
    for iteration in range(STEPS):
        rounded = current.astype(jnp.bfloat16)
        pieces = {0: rounded}
        for offset in (7, 6, 5, 4, 3, 2, 1, -1):
            pieces[offset] = shifted(rounded, "patch", offset)
        lower_side = jnp.concatenate([pieces[6 - segment] for segment in range(8)], axis=0)
        upper_side = jnp.concatenate([pieces[7 - segment] for segment in range(8)], axis=0)
        window_x = jnp.where(parity == 0, lower_side, upper_side).reshape(16, tile_size, col_width)
        totals = hessian_window(
            window_x, blocks, block_row - window_start, block_col - window_start, block_count
        )
        segments = totals.reshape(8, dev_rows, col_width)
        zero_rows = jnp.zeros((dev_rows, col_width), jnp.float32)
        applied = jnp.where(parity == 0, segments[6], segments[7])
        for offset in (1, -1, -2, -3, -4, -5, -6, -7):
            lower_seg = segments[offset + 6] if 0 <= offset + 6 <= 7 else zero_rows
            upper_seg = segments[offset + 7] if 0 <= offset + 7 <= 7 else zero_rows
            outgoing = jnp.where(parity == 0, lower_seg, upper_seg)
            applied = applied + shifted(outgoing, "patch", offset)
        current_all = lax.all_gather(current, "vec", axis=1, tiled=True)
        rayleigh = summed_over_patch(
            jnp.dot(
                current_all.T, applied, precision=exact_mode, preferred_element_type=jnp.float32
            )
            / total_rows
        )
        residual = applied - jnp.dot(
            current_all, rayleigh, precision=exact_mode, preferred_element_type=jnp.float32
        )
        update = current - step_rate * residual
        update_all = lax.all_gather(update, "vec", axis=1, tiled=True)
        gram_matrix = summed_over_patch(
            jnp.dot(
                update_all.T, update_all, precision=exact_mode, preferred_element_type=jnp.float32
            )
            / total_rows
        )
        factor = jnp.linalg.cholesky(gram_matrix)
        solved = lax.linalg.triangular_solve(
            factor, update_all, left_side=False, lower=True, transpose_a=True
        )
        current = lax.dynamic_slice_in_dim(solved, column_start, col_width, 1)
    return (current, residual)


def solution(mesh):
    in_specs = (P("patch", "vec"), P("patch", None, None), P("patch"), P("patch"), P("patch"))
    out_specs = (P("patch", "vec"), P("patch", "vec"))
    return jax.shard_map(shards, mesh=mesh, in_specs=in_specs, out_specs=out_specs, check_vma=False)
```

```python
import jax
import jax.numpy as jnp
from jax import lax
from jax.experimental import pallas as pl
from jax.experimental.pallas import tpu as pltpu
from jax.sharding import PartitionSpec as P

STEPS = 2


step_rate = 0.25
exact_mode = lax.Precision.HIGHEST


def shifted(block, axis, distance):
    devices = range(lax.axis_size(axis))
    route = [(i - distance, i) for i in devices if i - distance in devices]
    return lax.ppermute(block, axis, route)


def summed_over_patch(block, groups=((0, 2), (2, 2), (5, 2), (4, 1))):
    size = lax.axis_size("patch")
    me = lax.axis_index("patch")
    held = block
    for low, width in groups:
        ways = 1 << width
        part = held.shape[0] // ways
        digit = (me >> low) & (ways - 1)
        total = lax.dynamic_slice_in_dim(held, digit * part, part, 0)
        for e in range(1, ways):
            route = [(i, i ^ (e << low)) for i in range(size)]
            send = lax.dynamic_slice_in_dim(held, (digit ^ e) * part, part, 0)
            total = total + lax.ppermute(send, "patch", route)
        held = total
    for low, width in reversed(groups):
        ways = 1 << width
        digit = (me >> low) & (ways - 1)
        pieces = [held]
        for e in range(1, ways):
            route = [(i, i ^ (e << low)) for i in range(size)]
            pieces.append(lax.ppermute(held, "patch", route))
        order = jnp.arange(ways, dtype=jnp.int32) ^ digit
        held = jnp.take(jnp.stack(pieces), order, axis=0).reshape(-1, *held.shape[1:])
    return held


def tile_products(rows_ref, cols_ref, used_ref, tile_ref, x_ref, out_ref):
    slot = pl.program_id(0)

    @pl.when(slot == 0)
    def _():
        out_ref[...] = jnp.zeros_like(out_ref)

    @pl.when(slot < used_ref[0])
    def _():
        row = rows_ref[slot]
        col = cols_ref[slot]
        tile = tile_ref[0]
        weight = jnp.where(row == col, jnp.float32(0.5), jnp.float32(1.0))
        direct = jnp.dot(tile, x_ref[col], preferred_element_type=jnp.float32)
        out_ref[row] += direct * weight
        mirror = lax.dot_general(
            tile, x_ref[row], (((0,), (0,)), ((), ())), preferred_element_type=jnp.float32
        )
        out_ref[col] += mirror * weight


def hessian_window(window_x, blocks, rows_local, cols_local, used):
    slots, tile_size, _ = blocks.shape
    window_tiles, _, col_width = window_x.shape

    def tile_at(slot, rows, cols, used_ref):
        return (jnp.maximum(jnp.minimum(slot, used_ref[0] - 1), 0), 0, 0)

    def whole(slot, rows, cols, used_ref):
        return (0, 0, 0)

    grid_spec = pltpu.PrefetchScalarGridSpec(
        num_scalar_prefetch=3,
        grid=(slots,),
        in_specs=[
            pl.BlockSpec((1, tile_size, tile_size), tile_at),
            pl.BlockSpec((window_tiles, tile_size, col_width), whole),
        ],
        out_specs=pl.BlockSpec((window_tiles, tile_size, col_width), whole),
    )
    flops = 4 * slots * tile_size * tile_size * col_width
    return pl.pallas_call(
        tile_products,
        grid_spec=grid_spec,
        out_shape=jax.ShapeDtypeStruct((window_tiles, tile_size, col_width), jnp.float32),
        compiler_params=pltpu.CompilerParams(dimension_semantics=("arbitrary",)),
        cost_estimate=pl.CostEstimate(
            flops=flops,
            bytes_accessed=blocks.size * 2 + window_x.size * 2 + window_tiles * tile_size * col_width * 4,
            transcendentals=0,
        ),
    )(rows_local, cols_local, used, blocks, window_x)


def accumulate(window_x, totals, block_tiles, row_ids, col_ids, used_slots, window_start):
    group_total = (used_slots + 7) // 8

    def one_turn(group_index, partial_value):
        first_slot = group_index * 8
        chosen = lax.dynamic_slice_in_dim(block_tiles, first_slot, 8, 0)
        rows_here = lax.dynamic_slice_in_dim(row_ids, first_slot, 8, 0) - window_start
        cols_here = lax.dynamic_slice_in_dim(col_ids, first_slot, 8, 0) - window_start
        alive_mask = (first_slot + jnp.arange(8, dtype=jnp.int32) < used_slots).astype(jnp.float32)
        weight = (jnp.where(rows_here == cols_here, 0.5, 1.0).astype(jnp.float32) * alive_mask)[
            :, None, None
        ]
        direct = (
            jnp.einsum(
                "sab,sbk->sak", chosen, window_x[cols_here], preferred_element_type=jnp.float32
            )
            * weight
        )
        mirror = (
            jnp.einsum(
                "sba,sbk->sak", chosen, window_x[rows_here], preferred_element_type=jnp.float32
            )
            * weight
        )
        return partial_value.at[rows_here].add(direct).at[cols_here].add(mirror)

    return lax.fori_loop(0, group_total, one_turn, totals)


def shards(vectors, blocks, block_row, block_col, block_count):
    dev_rows, col_width = vectors.shape
    tile_size = blocks.shape[1]
    total_rows = dev_rows * lax.axis_size("patch")
    position = lax.axis_index("patch")
    parity = position % 2
    window_start = 2 * (position - 6 - parity)
    column_start = lax.axis_index("vec") * col_width
    used_slots = block_count[0]
    current = vectors
    residual = vectors
    for iteration in range(STEPS):
        rounded = current.astype(jnp.bfloat16)
        pieces = {0: rounded}
        for offset in (7, 6, 5, 4, 3, 2, 1, -1):
            pieces[offset] = shifted(rounded, "patch", offset)
        lower_side = jnp.concatenate([pieces[6 - segment] for segment in range(8)], axis=0)
        upper_side = jnp.concatenate([pieces[7 - segment] for segment in range(8)], axis=0)
        window_x = jnp.where(parity == 0, lower_side, upper_side).reshape(16, tile_size, col_width)
        totals = hessian_window(
            window_x, blocks, block_row - window_start, block_col - window_start, block_count
        )
        segments = totals.reshape(8, dev_rows, col_width)
        zero_rows = jnp.zeros((dev_rows, col_width), jnp.float32)
        applied = jnp.where(parity == 0, segments[6], segments[7])
        for offset in (1, -1, -2, -3, -4, -5, -6, -7):
            lower_seg = segments[offset + 6] if 0 <= offset + 6 <= 7 else zero_rows
            upper_seg = segments[offset + 7] if 0 <= offset + 7 <= 7 else zero_rows
            outgoing = jnp.where(parity == 0, lower_seg, upper_seg)
            applied = applied + shifted(outgoing, "patch", offset)
        current_all = lax.all_gather(current, "vec", axis=1, tiled=True)
        rayleigh = summed_over_patch(
            jnp.dot(
                current_all.T, applied, precision=exact_mode, preferred_element_type=jnp.float32
            )
            / total_rows
        )
        residual = applied - jnp.dot(
            current_all, rayleigh, precision=exact_mode, preferred_element_type=jnp.float32
        )
        update = current - step_rate * residual
        update_all = lax.all_gather(update, "vec", axis=1, tiled=True)
        gram_matrix = summed_over_patch(
            jnp.dot(
                update_all.T, update_all, precision=exact_mode, preferred_element_type=jnp.float32
            )
            / total_rows
        )
        factor = jnp.linalg.cholesky(gram_matrix)
        solved = lax.linalg.triangular_solve(
            factor, update_all, left_side=False, lower=True, transpose_a=True
        )
        current = lax.dynamic_slice_in_dim(solved, column_start, col_width, 1)
    return (current, residual)


def solution(mesh):
    in_specs = (P("patch", "vec"), P("patch", None, None), P("patch"), P("patch"), P("patch"))
    out_specs = (P("patch", "vec"), P("patch", "vec"))
    return jax.shard_map(shards, mesh=mesh, in_specs=in_specs, out_specs=out_specs, check_vma=False)
```

```python
import functools

import jax
import jax.numpy as jnp
from jax import lax
from jax.experimental import pallas as pl
from jax.experimental.pallas import tpu as pltpu
from jax.sharding import PartitionSpec as P

STEPS = 2


step_rate = 0.25
exact_mode = lax.Precision.HIGHEST


def shifted(block, axis, distance):
    devices = range(lax.axis_size(axis))
    route = [(i - distance, i) for i in devices if i - distance in devices]
    return lax.ppermute(block, axis, route)


ORDER = (0, 2, 5, 1, 3, 6, 4)

def exchange_sum(size, x_ref, out_ref, work_ref, recv_ref, final_ref, send_sems, recv_sems):
    me = lax.axis_index("patch")
    bits = [b for b in ORDER if (1 << b) < size]
    mesh_ids = pl.DeviceIdType.MESH

    def partner_of(b):
        side = (me // (1 << b)) % 2
        return side, me + (1 - 2 * side) * (1 << b)

    barrier = pltpu.get_barrier_semaphore()
    for b in bits:
        _, partner = partner_of(b)
        pl.semaphore_signal(barrier, 1, device_id={"patch": partner}, device_id_type=mesh_ids)
    pl.semaphore_wait(barrier, len(bits))
    work_ref[...] = x_ref[...]
    lo = 0
    span = work_ref.shape[0]
    recv_at = 0
    for k, b in enumerate(bits):
        span = span // 2
        side, partner = partner_of(b)
        keep = lo + side * span
        send = lo + (1 - side) * span
        copy = pltpu.make_async_remote_copy(
            src_ref=work_ref.at[pl.ds(send, span)],
            dst_ref=recv_ref.at[pl.ds(recv_at, span)],
            send_sem=send_sems.at[k],
            recv_sem=recv_sems.at[k],
            device_id={"patch": partner},
            device_id_type=mesh_ids,
        )
        copy.start()
        copy.wait()
        work_ref[pl.ds(keep, span)] = work_ref[pl.ds(keep, span)] + recv_ref[pl.ds(recv_at, span)]
        lo = keep
        recv_at += span
    final_ref[pl.ds(lo, span)] = work_ref[pl.ds(lo, span)]
    for j, b in enumerate(reversed(bits)):
        side, partner = partner_of(b)
        copy = pltpu.make_async_remote_copy(
            src_ref=final_ref.at[pl.ds(lo, span)],
            dst_ref=final_ref.at[pl.ds(lo, span)],
            send_sem=send_sems.at[len(bits) + j],
            recv_sem=recv_sems.at[len(bits) + j],
            device_id={"patch": partner},
            device_id_type=mesh_ids,
        )
        copy.start()
        copy.wait()
        lo = lo - side * span
        span = span * 2
    out_ref[...] = final_ref[...]


def summed_over_patch(block, collective):
    size = lax.axis_size("patch")
    rows, cols = block.shape
    lead = size
    flat = block.reshape(lead, (rows * cols) // (lead * 128), 128)
    steps = 2 * len([b for b in ORDER if (1 << b) < size])
    out = pl.pallas_call(
        functools.partial(exchange_sum, size),
        out_shape=jax.ShapeDtypeStruct(flat.shape, flat.dtype),
        in_specs=[pl.BlockSpec(memory_space=pltpu.VMEM)],
        out_specs=pl.BlockSpec(memory_space=pltpu.VMEM),
        scratch_shapes=[
            pltpu.VMEM(flat.shape, flat.dtype),
            pltpu.VMEM(flat.shape, flat.dtype),
            pltpu.VMEM(flat.shape, flat.dtype),
            pltpu.SemaphoreType.DMA((steps,)),
            pltpu.SemaphoreType.DMA((steps,)),
        ],
        compiler_params=pltpu.CompilerParams(collective_id=collective, has_side_effects=True),
    )(flat)
    return out.reshape(rows, cols)


def tile_products(rows_ref, cols_ref, used_ref, tile_ref, x_ref, out_ref):
    slot = pl.program_id(0)

    @pl.when(slot == 0)
    def _():
        out_ref[...] = jnp.zeros_like(out_ref)

    @pl.when(slot < used_ref[0])
    def _():
        row = rows_ref[slot]
        col = cols_ref[slot]
        tile = tile_ref[0]
        weight = jnp.where(row == col, jnp.float32(0.5), jnp.float32(1.0))
        direct = jnp.dot(tile, x_ref[col], preferred_element_type=jnp.float32)
        out_ref[row] += direct * weight
        mirror = lax.dot_general(
            tile, x_ref[row], (((0,), (0,)), ((), ())), preferred_element_type=jnp.float32
        )
        out_ref[col] += mirror * weight


def hessian_window(window_x, blocks, rows_local, cols_local, used):
    slots, tile_size, _ = blocks.shape
    window_tiles, _, col_width = window_x.shape

    def tile_at(slot, rows, cols, used_ref):
        return (jnp.maximum(jnp.minimum(slot, used_ref[0] - 1), 0), 0, 0)

    def whole(slot, rows, cols, used_ref):
        return (0, 0, 0)

    grid_spec = pltpu.PrefetchScalarGridSpec(
        num_scalar_prefetch=3,
        grid=(slots,),
        in_specs=[
            pl.BlockSpec((1, tile_size, tile_size), tile_at),
            pl.BlockSpec((window_tiles, tile_size, col_width), whole),
        ],
        out_specs=pl.BlockSpec((window_tiles, tile_size, col_width), whole),
    )
    flops = 4 * slots * tile_size * tile_size * col_width
    return pl.pallas_call(
        tile_products,
        grid_spec=grid_spec,
        out_shape=jax.ShapeDtypeStruct((window_tiles, tile_size, col_width), jnp.float32),
        compiler_params=pltpu.CompilerParams(dimension_semantics=("arbitrary",)),
        cost_estimate=pl.CostEstimate(
            flops=flops,
            bytes_accessed=blocks.size * 2 + window_x.size * 2 + window_tiles * tile_size * col_width * 4,
            transcendentals=0,
        ),
    )(rows_local, cols_local, used, blocks, window_x)


def accumulate(window_x, totals, block_tiles, row_ids, col_ids, used_slots, window_start):
    group_total = (used_slots + 7) // 8

    def one_turn(group_index, partial_value):
        first_slot = group_index * 8
        chosen = lax.dynamic_slice_in_dim(block_tiles, first_slot, 8, 0)
        rows_here = lax.dynamic_slice_in_dim(row_ids, first_slot, 8, 0) - window_start
        cols_here = lax.dynamic_slice_in_dim(col_ids, first_slot, 8, 0) - window_start
        alive_mask = (first_slot + jnp.arange(8, dtype=jnp.int32) < used_slots).astype(jnp.float32)
        weight = (jnp.where(rows_here == cols_here, 0.5, 1.0).astype(jnp.float32) * alive_mask)[
            :, None, None
        ]
        direct = (
            jnp.einsum(
                "sab,sbk->sak", chosen, window_x[cols_here], preferred_element_type=jnp.float32
            )
            * weight
        )
        mirror = (
            jnp.einsum(
                "sba,sbk->sak", chosen, window_x[rows_here], preferred_element_type=jnp.float32
            )
            * weight
        )
        return partial_value.at[rows_here].add(direct).at[cols_here].add(mirror)

    return lax.fori_loop(0, group_total, one_turn, totals)


def shards(vectors, blocks, block_row, block_col, block_count):
    dev_rows, col_width = vectors.shape
    tile_size = blocks.shape[1]
    total_rows = dev_rows * lax.axis_size("patch")
    position = lax.axis_index("patch")
    parity = position % 2
    window_start = 2 * (position - 6 - parity)
    column_start = lax.axis_index("vec") * col_width
    used_slots = block_count[0]
    current = vectors
    residual = vectors
    for iteration in range(STEPS):
        rounded = current.astype(jnp.bfloat16)
        pieces = {0: rounded}
        for offset in (7, 6, 5, 4, 3, 2, 1, -1):
            pieces[offset] = shifted(rounded, "patch", offset)
        lower_side = jnp.concatenate([pieces[6 - segment] for segment in range(8)], axis=0)
        upper_side = jnp.concatenate([pieces[7 - segment] for segment in range(8)], axis=0)
        window_x = jnp.where(parity == 0, lower_side, upper_side).reshape(16, tile_size, col_width)
        totals = hessian_window(
            window_x, blocks, block_row - window_start, block_col - window_start, block_count
        )
        segments = totals.reshape(8, dev_rows, col_width)
        zero_rows = jnp.zeros((dev_rows, col_width), jnp.float32)
        applied = jnp.where(parity == 0, segments[6], segments[7])
        for offset in (1, -1, -2, -3, -4, -5, -6, -7):
            lower_seg = segments[offset + 6] if 0 <= offset + 6 <= 7 else zero_rows
            upper_seg = segments[offset + 7] if 0 <= offset + 7 <= 7 else zero_rows
            outgoing = jnp.where(parity == 0, lower_seg, upper_seg)
            applied = applied + shifted(outgoing, "patch", offset)
        current_all = lax.all_gather(current, "vec", axis=1, tiled=True)
        rayleigh = summed_over_patch(
            jnp.dot(
                current_all.T, applied, precision=exact_mode, preferred_element_type=jnp.float32
            )
            / total_rows,
            0,
        )
        residual = applied - jnp.dot(
            current_all, rayleigh, precision=exact_mode, preferred_element_type=jnp.float32
        )
        update = current - step_rate * residual
        update_all = lax.all_gather(update, "vec", axis=1, tiled=True)
        gram_matrix = summed_over_patch(
            jnp.dot(
                update_all.T, update_all, precision=exact_mode, preferred_element_type=jnp.float32
            )
            / total_rows,
            1,
        )
        factor = jnp.linalg.cholesky(gram_matrix)
        solved = lax.linalg.triangular_solve(
            factor, update_all, left_side=False, lower=True, transpose_a=True
        )
        current = lax.dynamic_slice_in_dim(solved, column_start, col_width, 1)
    return (current, residual)


def solution(mesh):
    in_specs = (P("patch", "vec"), P("patch", None, None), P("patch"), P("patch"), P("patch"))
    out_specs = (P("patch", "vec"), P("patch", "vec"))
    return jax.shard_map(shards, mesh=mesh, in_specs=in_specs, out_specs=out_specs, check_vma=False)
```

```python
import functools

import jax
import jax.numpy as jnp
from jax import lax
from jax.experimental import pallas as pl
from jax.experimental.pallas import tpu as pltpu
from jax.sharding import PartitionSpec as P

STEPS = 2


step_rate = 0.25
exact_mode = lax.Precision.HIGHEST


def shifted(block, axis, distance):
    devices = range(lax.axis_size(axis))
    route = [(i - distance, i) for i in devices if i - distance in devices]
    return lax.ppermute(block, axis, route)


GROUPS = ((0, 2), (2, 2), (5, 2), (4, 1))


def digit_groups(size):
    nbits = size.bit_length() - 1
    return [(low, min(width, nbits - low)) for low, width in GROUPS if low < nbits]


def flipped(digit, e, width):
    total = 0
    for bit in range(width):
        total = total + ((digit // (1 << bit) + e // (1 << bit)) % 2) * (1 << bit)
    return total


def exchange_sum(size, x_ref, out_ref, work_ref, recv_ref, final_ref, send_sems, recv_sems):
    me = lax.axis_index("patch")
    groups = digit_groups(size)
    mesh_ids = pl.DeviceIdType.MESH

    def digit_of(low, width):
        return (me // (1 << low)) % (1 << width)

    def partner_of(low, width, e):
        digit = digit_of(low, width)
        return me + (flipped(digit, e, width) - digit) * (1 << low)

    barrier = pltpu.get_barrier_semaphore()
    greeted = 0
    for low, width in groups:
        for e in range(1, 1 << width):
            pl.semaphore_signal(
                barrier, 1, device_id={"patch": partner_of(low, width, e)}, device_id_type=mesh_ids
            )
            greeted += 1
    pl.semaphore_wait(barrier, greeted)
    work_ref[...] = x_ref[...]
    lo = 0
    span = work_ref.shape[0]
    recv_at = 0
    sem = 0
    for low, width in groups:
        ways = 1 << width
        span = span // ways
        digit = digit_of(low, width)
        copies = []
        for e in range(1, ways):
            copy = pltpu.make_async_remote_copy(
                src_ref=work_ref.at[pl.ds(lo + flipped(digit, e, width) * span, span)],
                dst_ref=recv_ref.at[pl.ds(recv_at + (e - 1) * span, span)],
                send_sem=send_sems.at[sem],
                recv_sem=recv_sems.at[sem],
                device_id={"patch": partner_of(low, width, e)},
                device_id_type=mesh_ids,
            )
            copy.start()
            copies.append(copy)
            sem += 1
        for copy in copies:
            copy.wait()
        keep = lo + digit * span
        total = work_ref[pl.ds(keep, span)]
        for e in range(1, ways):
            total = total + recv_ref[pl.ds(recv_at + (e - 1) * span, span)]
        work_ref[pl.ds(keep, span)] = total
        lo = keep
        recv_at += (ways - 1) * span
    final_ref[pl.ds(lo, span)] = work_ref[pl.ds(lo, span)]
    for low, width in reversed(groups):
        ways = 1 << width
        digit = digit_of(low, width)
        copies = []
        for e in range(1, ways):
            copy = pltpu.make_async_remote_copy(
                src_ref=final_ref.at[pl.ds(lo, span)],
                dst_ref=final_ref.at[pl.ds(lo, span)],
                send_sem=send_sems.at[sem],
                recv_sem=recv_sems.at[sem],
                device_id={"patch": partner_of(low, width, e)},
                device_id_type=mesh_ids,
            )
            copy.start()
            copies.append(copy)
            sem += 1
        for copy in copies:
            copy.wait()
        lo = lo - digit * span
        span = span * ways
    out_ref[...] = final_ref[...]


def summed_over_patch(block, collective):
    size = lax.axis_size("patch")
    rows, cols = block.shape
    flat = block.reshape(size, (rows * cols) // (size * 128), 128)
    steps = 2 * sum((1 << width) - 1 for _, width in digit_groups(size))
    out = pl.pallas_call(
        functools.partial(exchange_sum, size),
        out_shape=jax.ShapeDtypeStruct(flat.shape, flat.dtype),
        in_specs=[pl.BlockSpec(memory_space=pltpu.VMEM)],
        out_specs=pl.BlockSpec(memory_space=pltpu.VMEM),
        scratch_shapes=[
            pltpu.VMEM(flat.shape, flat.dtype),
            pltpu.VMEM(flat.shape, flat.dtype),
            pltpu.VMEM(flat.shape, flat.dtype),
            pltpu.SemaphoreType.DMA((steps,)),
            pltpu.SemaphoreType.DMA((steps,)),
        ],
        compiler_params=pltpu.CompilerParams(collective_id=collective, has_side_effects=True),
    )(flat)
    return out.reshape(rows, cols)


def tile_products(rows_ref, cols_ref, used_ref, tile_ref, x_ref, out_ref):
    slot = pl.program_id(0)

    @pl.when(slot == 0)
    def _():
        out_ref[...] = jnp.zeros_like(out_ref)

    @pl.when(slot < used_ref[0])
    def _():
        row = rows_ref[slot]
        col = cols_ref[slot]
        tile = tile_ref[0]
        weight = jnp.where(row == col, jnp.float32(0.5), jnp.float32(1.0))
        direct = jnp.dot(tile, x_ref[col], preferred_element_type=jnp.float32)
        out_ref[row] += direct * weight
        mirror = lax.dot_general(
            tile, x_ref[row], (((0,), (0,)), ((), ())), preferred_element_type=jnp.float32
        )
        out_ref[col] += mirror * weight


def hessian_window(window_x, blocks, rows_local, cols_local, used):
    slots, tile_size, _ = blocks.shape
    window_tiles, _, col_width = window_x.shape

    def tile_at(slot, rows, cols, used_ref):
        return (jnp.maximum(jnp.minimum(slot, used_ref[0] - 1), 0), 0, 0)

    def whole(slot, rows, cols, used_ref):
        return (0, 0, 0)

    grid_spec = pltpu.PrefetchScalarGridSpec(
        num_scalar_prefetch=3,
        grid=(slots,),
        in_specs=[
            pl.BlockSpec((1, tile_size, tile_size), tile_at),
            pl.BlockSpec((window_tiles, tile_size, col_width), whole),
        ],
        out_specs=pl.BlockSpec((window_tiles, tile_size, col_width), whole),
    )
    flops = 4 * slots * tile_size * tile_size * col_width
    return pl.pallas_call(
        tile_products,
        grid_spec=grid_spec,
        out_shape=jax.ShapeDtypeStruct((window_tiles, tile_size, col_width), jnp.float32),
        compiler_params=pltpu.CompilerParams(dimension_semantics=("arbitrary",)),
        cost_estimate=pl.CostEstimate(
            flops=flops,
            bytes_accessed=blocks.size * 2 + window_x.size * 2 + window_tiles * tile_size * col_width * 4,
            transcendentals=0,
        ),
    )(rows_local, cols_local, used, blocks, window_x)


def accumulate(window_x, totals, block_tiles, row_ids, col_ids, used_slots, window_start):
    group_total = (used_slots + 7) // 8

    def one_turn(group_index, partial_value):
        first_slot = group_index * 8
        chosen = lax.dynamic_slice_in_dim(block_tiles, first_slot, 8, 0)
        rows_here = lax.dynamic_slice_in_dim(row_ids, first_slot, 8, 0) - window_start
        cols_here = lax.dynamic_slice_in_dim(col_ids, first_slot, 8, 0) - window_start
        alive_mask = (first_slot + jnp.arange(8, dtype=jnp.int32) < used_slots).astype(jnp.float32)
        weight = (jnp.where(rows_here == cols_here, 0.5, 1.0).astype(jnp.float32) * alive_mask)[
            :, None, None
        ]
        direct = (
            jnp.einsum(
                "sab,sbk->sak", chosen, window_x[cols_here], preferred_element_type=jnp.float32
            )
            * weight
        )
        mirror = (
            jnp.einsum(
                "sba,sbk->sak", chosen, window_x[rows_here], preferred_element_type=jnp.float32
            )
            * weight
        )
        return partial_value.at[rows_here].add(direct).at[cols_here].add(mirror)

    return lax.fori_loop(0, group_total, one_turn, totals)


def shards(vectors, blocks, block_row, block_col, block_count):
    dev_rows, col_width = vectors.shape
    tile_size = blocks.shape[1]
    total_rows = dev_rows * lax.axis_size("patch")
    position = lax.axis_index("patch")
    parity = position % 2
    window_start = 2 * (position - 6 - parity)
    column_start = lax.axis_index("vec") * col_width
    used_slots = block_count[0]
    current = vectors
    residual = vectors
    for iteration in range(STEPS):
        rounded = current.astype(jnp.bfloat16)
        pieces = {0: rounded}
        for offset in (7, 6, 5, 4, 3, 2, 1, -1):
            pieces[offset] = shifted(rounded, "patch", offset)
        lower_side = jnp.concatenate([pieces[6 - segment] for segment in range(8)], axis=0)
        upper_side = jnp.concatenate([pieces[7 - segment] for segment in range(8)], axis=0)
        window_x = jnp.where(parity == 0, lower_side, upper_side).reshape(16, tile_size, col_width)
        totals = hessian_window(
            window_x, blocks, block_row - window_start, block_col - window_start, block_count
        )
        segments = totals.reshape(8, dev_rows, col_width)
        zero_rows = jnp.zeros((dev_rows, col_width), jnp.float32)
        applied = jnp.where(parity == 0, segments[6], segments[7])
        for offset in (1, -1, -2, -3, -4, -5, -6, -7):
            lower_seg = segments[offset + 6] if 0 <= offset + 6 <= 7 else zero_rows
            upper_seg = segments[offset + 7] if 0 <= offset + 7 <= 7 else zero_rows
            outgoing = jnp.where(parity == 0, lower_seg, upper_seg)
            applied = applied + shifted(outgoing, "patch", offset)
        current_all = lax.all_gather(current, "vec", axis=1, tiled=True)
        rayleigh = summed_over_patch(
            jnp.dot(
                current_all.T, applied, precision=exact_mode, preferred_element_type=jnp.float32
            )
            / total_rows,
            0,
        )
        residual = applied - jnp.dot(
            current_all, rayleigh, precision=exact_mode, preferred_element_type=jnp.float32
        )
        update = current - step_rate * residual
        update_all = lax.all_gather(update, "vec", axis=1, tiled=True)
        gram_matrix = summed_over_patch(
            jnp.dot(
                update_all.T, update_all, precision=exact_mode, preferred_element_type=jnp.float32
            )
            / total_rows,
            1,
        )
        factor = jnp.linalg.cholesky(gram_matrix)
        solved = lax.linalg.triangular_solve(
            factor, update_all, left_side=False, lower=True, transpose_a=True
        )
        current = lax.dynamic_slice_in_dim(solved, column_start, col_width, 1)
    return (current, residual)


def solution(mesh):
    in_specs = (P("patch", "vec"), P("patch", None, None), P("patch"), P("patch"), P("patch"))
    out_specs = (P("patch", "vec"), P("patch", "vec"))
    return jax.shard_map(shards, mesh=mesh, in_specs=in_specs, out_specs=out_specs, check_vma=False)
```

```python
import functools

import jax
import jax.numpy as jnp
from jax import lax
from jax.experimental import pallas as pl
from jax.experimental.pallas import tpu as pltpu
from jax.sharding import PartitionSpec as P

STEPS = 2


step_rate = 0.25
exact_mode = lax.Precision.HIGHEST


def shifted(block, axis, distance):
    devices = range(lax.axis_size(axis))
    route = [(i - distance, i) for i in devices if i - distance in devices]
    return lax.ppermute(block, axis, route)


GROUPS = ((0, 2), (2, 2), (5, 2), (4, 1))


def digit_groups(size):
    nbits = size.bit_length() - 1
    return [(low, min(width, nbits - low)) for low, width in GROUPS if low < nbits]


def flipped(digit, e, width):
    total = 0
    for bit in range(width):
        total = total + ((digit // (1 << bit) + e // (1 << bit)) % 2) * (1 << bit)
    return total


def exchange_sum(size, x_ref, out_ref, work_ref, recv_ref, final_ref, send_sems, recv_sems):
    me = lax.axis_index("patch")
    groups = digit_groups(size)
    mesh_ids = pl.DeviceIdType.MESH

    def digit_of(low, width):
        return (me // (1 << low)) % (1 << width)

    def partner_of(low, width, e):
        digit = digit_of(low, width)
        return me + (flipped(digit, e, width) - digit) * (1 << low)

    barrier = pltpu.get_barrier_semaphore()
    greeted = 0
    for low, width in groups:
        for e in range(1, 1 << width):
            pl.semaphore_signal(
                barrier, 1, device_id={"patch": partner_of(low, width, e)}, device_id_type=mesh_ids
            )
            greeted += 1
    pl.semaphore_wait(barrier, greeted)
    work_ref[...] = x_ref[...]
    lo = 0
    span = work_ref.shape[0]
    recv_at = 0
    sem = 0
    for low, width in groups:
        ways = 1 << width
        span = span // ways
        digit = digit_of(low, width)
        copies = []
        for e in range(1, ways):
            copy = pltpu.make_async_remote_copy(
                src_ref=work_ref.at[pl.ds(lo + flipped(digit, e, width) * span, span)],
                dst_ref=recv_ref.at[pl.ds(recv_at + (e - 1) * span, span)],
                send_sem=send_sems.at[sem],
                recv_sem=recv_sems.at[sem],
                device_id={"patch": partner_of(low, width, e)},
                device_id_type=mesh_ids,
            )
            copy.start()
            copies.append(copy)
            sem += 1
        for copy in copies:
            copy.wait()
        keep = lo + digit * span
        total = work_ref[pl.ds(keep, span)]
        for e in range(1, ways):
            total = total + recv_ref[pl.ds(recv_at + (e - 1) * span, span)]
        work_ref[pl.ds(keep, span)] = total
        lo = keep
        recv_at += (ways - 1) * span
    final_ref[pl.ds(lo, span)] = work_ref[pl.ds(lo, span)]
    for low, width in reversed(groups):
        ways = 1 << width
        digit = digit_of(low, width)
        copies = []
        for e in range(1, ways):
            copy = pltpu.make_async_remote_copy(
                src_ref=final_ref.at[pl.ds(lo, span)],
                dst_ref=final_ref.at[pl.ds(lo, span)],
                send_sem=send_sems.at[sem],
                recv_sem=recv_sems.at[sem],
                device_id={"patch": partner_of(low, width, e)},
                device_id_type=mesh_ids,
            )
            copy.start()
            copies.append(copy)
            sem += 1
        for copy in copies:
            copy.wait()
        lo = lo - digit * span
        span = span * ways
    out_ref[...] = final_ref[...]


def summed_over_patch(block, collective):
    size = lax.axis_size("patch")
    rows, cols = block.shape
    flat = block.reshape(size, (rows * cols) // (size * 128), 128)
    steps = 2 * sum((1 << width) - 1 for _, width in digit_groups(size))
    out = pl.pallas_call(
        functools.partial(exchange_sum, size),
        out_shape=jax.ShapeDtypeStruct(flat.shape, flat.dtype),
        in_specs=[pl.BlockSpec(memory_space=pltpu.VMEM)],
        out_specs=pl.BlockSpec(memory_space=pltpu.VMEM),
        scratch_shapes=[
            pltpu.VMEM(flat.shape, flat.dtype),
            pltpu.VMEM(flat.shape, flat.dtype),
            pltpu.VMEM(flat.shape, flat.dtype),
            pltpu.SemaphoreType.DMA((steps,)),
            pltpu.SemaphoreType.DMA((steps,)),
        ],
        compiler_params=pltpu.CompilerParams(collective_id=collective, has_side_effects=True),
    )(flat)
    return out.reshape(rows, cols)


SHIFTS = (1, -1, -2, -3, -4, -5, -6, -7)


def gather_partials(size, own_ref, parts_ref, out_ref, recv_ref, send_sems, recv_sems):
    me = lax.axis_index("patch")
    mesh_ids = pl.DeviceIdType.MESH
    barrier = pltpu.get_barrier_semaphore()
    targets = 0
    for shift in SHIFTS:
        source = me - shift
        target = me + shift

        @pl.when((source >= 0) & (source < size))
        def _():
            pl.semaphore_signal(barrier, 1, device_id={"patch": source}, device_id_type=mesh_ids)

        targets = targets + ((target >= 0) & (target < size)).astype(jnp.int32)
    for slot, shift in enumerate(SHIFTS):
        source = me - shift

        @pl.when((source < 0) | (source >= size))
        def _():
            recv_ref[slot] = jnp.zeros(recv_ref.shape[1:], recv_ref.dtype)

    pl.semaphore_wait(barrier, targets)
    copies = []
    for slot, shift in enumerate(SHIFTS):
        target = me + shift
        source = me - shift
        copy = pltpu.make_async_remote_copy(
            src_ref=parts_ref.at[slot],
            dst_ref=recv_ref.at[slot],
            send_sem=send_sems.at[slot],
            recv_sem=recv_sems.at[slot],
            device_id={"patch": target},
            device_id_type=mesh_ids,
        )
        sends = (target >= 0) & (target < size)
        gets = (source >= 0) & (source < size)

        @pl.when(sends)
        def _():
            copy.start()

        copies.append((copy, sends, gets))
    total = own_ref[...]
    for slot, (copy, sends, gets) in enumerate(copies):

        @pl.when(gets)
        def _():
            copy.wait_recv()

        total = total + jnp.where(gets, recv_ref[slot], jnp.float32(0.0))
    out_ref[...] = total
    for copy, sends, gets in copies:

        @pl.when(sends)
        def _():
            copy.wait_send()


def summed_partials(own, parts):
    size = lax.axis_size("patch")
    return pl.pallas_call(
        functools.partial(gather_partials, size),
        out_shape=jax.ShapeDtypeStruct(own.shape, own.dtype),
        in_specs=[pl.BlockSpec(memory_space=pltpu.VMEM)] * 2,
        out_specs=pl.BlockSpec(memory_space=pltpu.VMEM),
        scratch_shapes=[
            pltpu.VMEM(parts.shape, parts.dtype),
            pltpu.SemaphoreType.DMA((len(SHIFTS),)),
            pltpu.SemaphoreType.DMA((len(SHIFTS),)),
        ],
        compiler_params=pltpu.CompilerParams(collective_id=2, has_side_effects=True),
    )(own, parts)


def tile_products(rows_ref, cols_ref, used_ref, tile_ref, x_ref, out_ref):
    slot = pl.program_id(0)

    @pl.when(slot == 0)
    def _():
        out_ref[...] = jnp.zeros_like(out_ref)

    @pl.when(slot < used_ref[0])
    def _():
        row = rows_ref[slot]
        col = cols_ref[slot]
        tile = tile_ref[0]
        weight = jnp.where(row == col, jnp.float32(0.5), jnp.float32(1.0))
        direct = jnp.dot(tile, x_ref[col], preferred_element_type=jnp.float32)
        out_ref[row] += direct * weight
        mirror = lax.dot_general(
            tile, x_ref[row], (((0,), (0,)), ((), ())), preferred_element_type=jnp.float32
        )
        out_ref[col] += mirror * weight


def hessian_window(window_x, blocks, rows_local, cols_local, used):
    slots, tile_size, _ = blocks.shape
    window_tiles, _, col_width = window_x.shape

    def tile_at(slot, rows, cols, used_ref):
        return (jnp.maximum(jnp.minimum(slot, used_ref[0] - 1), 0), 0, 0)

    def whole(slot, rows, cols, used_ref):
        return (0, 0, 0)

    grid_spec = pltpu.PrefetchScalarGridSpec(
        num_scalar_prefetch=3,
        grid=(slots,),
        in_specs=[
            pl.BlockSpec((1, tile_size, tile_size), tile_at),
            pl.BlockSpec((window_tiles, tile_size, col_width), whole),
        ],
        out_specs=pl.BlockSpec((window_tiles, tile_size, col_width), whole),
    )
    flops = 4 * slots * tile_size * tile_size * col_width
    return pl.pallas_call(
        tile_products,
        grid_spec=grid_spec,
        out_shape=jax.ShapeDtypeStruct((window_tiles, tile_size, col_width), jnp.float32),
        compiler_params=pltpu.CompilerParams(dimension_semantics=("arbitrary",)),
        cost_estimate=pl.CostEstimate(
            flops=flops,
            bytes_accessed=blocks.size * 2 + window_x.size * 2 + window_tiles * tile_size * col_width * 4,
            transcendentals=0,
        ),
    )(rows_local, cols_local, used, blocks, window_x)


def accumulate(window_x, totals, block_tiles, row_ids, col_ids, used_slots, window_start):
    group_total = (used_slots + 7) // 8

    def one_turn(group_index, partial_value):
        first_slot = group_index * 8
        chosen = lax.dynamic_slice_in_dim(block_tiles, first_slot, 8, 0)
        rows_here = lax.dynamic_slice_in_dim(row_ids, first_slot, 8, 0) - window_start
        cols_here = lax.dynamic_slice_in_dim(col_ids, first_slot, 8, 0) - window_start
        alive_mask = (first_slot + jnp.arange(8, dtype=jnp.int32) < used_slots).astype(jnp.float32)
        weight = (jnp.where(rows_here == cols_here, 0.5, 1.0).astype(jnp.float32) * alive_mask)[
            :, None, None
        ]
        direct = (
            jnp.einsum(
                "sab,sbk->sak", chosen, window_x[cols_here], preferred_element_type=jnp.float32
            )
            * weight
        )
        mirror = (
            jnp.einsum(
                "sba,sbk->sak", chosen, window_x[rows_here], preferred_element_type=jnp.float32
            )
            * weight
        )
        return partial_value.at[rows_here].add(direct).at[cols_here].add(mirror)

    return lax.fori_loop(0, group_total, one_turn, totals)


def shards(vectors, blocks, block_row, block_col, block_count):
    dev_rows, col_width = vectors.shape
    tile_size = blocks.shape[1]
    total_rows = dev_rows * lax.axis_size("patch")
    position = lax.axis_index("patch")
    parity = position % 2
    window_start = 2 * (position - 6 - parity)
    column_start = lax.axis_index("vec") * col_width
    used_slots = block_count[0]
    current = vectors
    residual = vectors
    for iteration in range(STEPS):
        rounded = current.astype(jnp.bfloat16)
        pieces = {0: rounded}
        for offset in (7, 6, 5, 4, 3, 2, 1, -1):
            pieces[offset] = shifted(rounded, "patch", offset)
        lower_side = jnp.concatenate([pieces[6 - segment] for segment in range(8)], axis=0)
        upper_side = jnp.concatenate([pieces[7 - segment] for segment in range(8)], axis=0)
        window_x = jnp.where(parity == 0, lower_side, upper_side).reshape(16, tile_size, col_width)
        totals = hessian_window(
            window_x, blocks, block_row - window_start, block_col - window_start, block_count
        )
        segments = totals.reshape(8, dev_rows, col_width)
        zero_rows = jnp.zeros((dev_rows, col_width), jnp.float32)
        applied = jnp.where(parity == 0, segments[6], segments[7])
        outgoing = []
        for offset in SHIFTS:
            lower_seg = segments[offset + 6] if 0 <= offset + 6 <= 7 else zero_rows
            upper_seg = segments[offset + 7] if 0 <= offset + 7 <= 7 else zero_rows
            outgoing.append(jnp.where(parity == 0, lower_seg, upper_seg))
        applied = summed_partials(applied, jnp.stack(outgoing))
        current_all = lax.all_gather(current, "vec", axis=1, tiled=True)
        rayleigh = summed_over_patch(
            jnp.dot(
                current_all.T, applied, precision=exact_mode, preferred_element_type=jnp.float32
            )
            / total_rows,
            0,
        )
        residual = applied - jnp.dot(
            current_all, rayleigh, precision=exact_mode, preferred_element_type=jnp.float32
        )
        update = current - step_rate * residual
        update_all = lax.all_gather(update, "vec", axis=1, tiled=True)
        gram_matrix = summed_over_patch(
            jnp.dot(
                update_all.T, update_all, precision=exact_mode, preferred_element_type=jnp.float32
            )
            / total_rows,
            1,
        )
        factor = jnp.linalg.cholesky(gram_matrix)
        solved = lax.linalg.triangular_solve(
            factor, update_all, left_side=False, lower=True, transpose_a=True
        )
        current = lax.dynamic_slice_in_dim(solved, column_start, col_width, 1)
    return (current, residual)


def solution(mesh):
    in_specs = (P("patch", "vec"), P("patch", None, None), P("patch"), P("patch"), P("patch"))
    out_specs = (P("patch", "vec"), P("patch", "vec"))
    return jax.shard_map(shards, mesh=mesh, in_specs=in_specs, out_specs=out_specs, check_vma=False)
```

```python
import functools

import jax
import jax.numpy as jnp
from jax import lax
from jax.experimental import pallas as pl
from jax.experimental.pallas import tpu as pltpu
from jax.sharding import PartitionSpec as P

STEPS = 2


step_rate = 0.25
exact_mode = lax.Precision.HIGHEST


def shifted(block, axis, distance):
    devices = range(lax.axis_size(axis))
    route = [(i - distance, i) for i in devices if i - distance in devices]
    return lax.ppermute(block, axis, route)


GROUPS = ((0, 2), (2, 2), (5, 2), (4, 1))


def digit_groups(size):
    nbits = size.bit_length() - 1
    return [(low, min(width, nbits - low)) for low, width in GROUPS if low < nbits]


def flipped(digit, e, width):
    total = 0
    for bit in range(width):
        total = total + ((digit // (1 << bit) + e // (1 << bit)) % 2) * (1 << bit)
    return total


def exchange_sum(size, x_ref, out_ref, work_ref, recv_ref, final_ref, send_sems, recv_sems):
    me = lax.axis_index("patch")
    groups = digit_groups(size)
    mesh_ids = pl.DeviceIdType.MESH

    def digit_of(low, width):
        return (me // (1 << low)) % (1 << width)

    def partner_of(low, width, e):
        digit = digit_of(low, width)
        return me + (flipped(digit, e, width) - digit) * (1 << low)

    barrier = pltpu.get_barrier_semaphore()
    greeted = 0
    for low, width in groups:
        for e in range(1, 1 << width):
            pl.semaphore_signal(
                barrier, 1, device_id={"patch": partner_of(low, width, e)}, device_id_type=mesh_ids
            )
            greeted += 1
    pl.semaphore_wait(barrier, greeted)
    work_ref[...] = x_ref[...]
    lo = 0
    span = work_ref.shape[0]
    recv_at = 0
    sem = 0
    for low, width in groups:
        ways = 1 << width
        span = span // ways
        digit = digit_of(low, width)
        copies = []
        for e in range(1, ways):
            copy = pltpu.make_async_remote_copy(
                src_ref=work_ref.at[pl.ds(lo + flipped(digit, e, width) * span, span)],
                dst_ref=recv_ref.at[pl.ds(recv_at + (e - 1) * span, span)],
                send_sem=send_sems.at[sem],
                recv_sem=recv_sems.at[sem],
                device_id={"patch": partner_of(low, width, e)},
                device_id_type=mesh_ids,
            )
            copy.start()
            copies.append(copy)
            sem += 1
        for copy in copies:
            copy.wait()
        keep = lo + digit * span
        total = work_ref[pl.ds(keep, span)]
        for e in range(1, ways):
            total = total + recv_ref[pl.ds(recv_at + (e - 1) * span, span)]
        work_ref[pl.ds(keep, span)] = total
        lo = keep
        recv_at += (ways - 1) * span
    final_ref[pl.ds(lo, span)] = work_ref[pl.ds(lo, span)]
    for low, width in reversed(groups):
        ways = 1 << width
        digit = digit_of(low, width)
        copies = []
        for e in range(1, ways):
            copy = pltpu.make_async_remote_copy(
                src_ref=final_ref.at[pl.ds(lo, span)],
                dst_ref=final_ref.at[pl.ds(lo, span)],
                send_sem=send_sems.at[sem],
                recv_sem=recv_sems.at[sem],
                device_id={"patch": partner_of(low, width, e)},
                device_id_type=mesh_ids,
            )
            copy.start()
            copies.append(copy)
            sem += 1
        for copy in copies:
            copy.wait()
        lo = lo - digit * span
        span = span * ways
    out_ref[...] = final_ref[...]


def summed_over_patch(block, collective):
    size = lax.axis_size("patch")
    rows, cols = block.shape
    flat = block.reshape(size, (rows * cols) // (size * 128), 128)
    steps = 2 * sum((1 << width) - 1 for _, width in digit_groups(size))
    out = pl.pallas_call(
        functools.partial(exchange_sum, size),
        out_shape=jax.ShapeDtypeStruct(flat.shape, flat.dtype),
        in_specs=[pl.BlockSpec(memory_space=pltpu.VMEM)],
        out_specs=pl.BlockSpec(memory_space=pltpu.VMEM),
        scratch_shapes=[
            pltpu.VMEM(flat.shape, flat.dtype),
            pltpu.VMEM(flat.shape, flat.dtype),
            pltpu.VMEM(flat.shape, flat.dtype),
            pltpu.SemaphoreType.DMA((steps,)),
            pltpu.SemaphoreType.DMA((steps,)),
        ],
        compiler_params=pltpu.CompilerParams(collective_id=collective, has_side_effects=True),
    )(flat)
    return out.reshape(rows, cols)


def tile_products(part, base, rows_ref, cols_ref, used_ref, tile_ref, x_ref, out_ref):
    slot = pl.program_id(0)

    @pl.when(slot == 0)
    def _():
        out_ref[...] = jnp.zeros_like(out_ref)

    @pl.when(slot < used_ref[0])
    def _():
        row = rows_ref[slot]
        col = cols_ref[slot]
        tile = tile_ref[0]
        weight = jnp.where(row == col, jnp.float32(0.5), jnp.float32(1.0))
        if part == "direct":
            direct = jnp.dot(tile, x_ref[col], preferred_element_type=jnp.float32)
            out_ref[row] += direct * weight
        else:
            mirror = lax.dot_general(
                tile, x_ref[row - base], (((0,), (0,)), ((), ())), preferred_element_type=jnp.float32
            )
            out_ref[col] += mirror * weight


def hessian_window(window_x, blocks, rows_local, cols_local, used, part, window_tiles):
    slots, tile_size, _ = blocks.shape
    held_tiles, _, col_width = window_x.shape

    def tile_at(slot, rows, cols, used_ref):
        return (jnp.maximum(jnp.minimum(slot, used_ref[0] - 1), 0), 0, 0)

    def whole(slot, rows, cols, used_ref):
        return (0, 0, 0)

    grid_spec = pltpu.PrefetchScalarGridSpec(
        num_scalar_prefetch=3,
        grid=(slots,),
        in_specs=[
            pl.BlockSpec((1, tile_size, tile_size), tile_at),
            pl.BlockSpec((held_tiles, tile_size, col_width), whole),
        ],
        out_specs=pl.BlockSpec((window_tiles, tile_size, col_width), whole),
    )
    flops = 2 * slots * tile_size * tile_size * col_width
    return pl.pallas_call(
        functools.partial(tile_products, part, window_tiles - held_tiles),
        grid_spec=grid_spec,
        out_shape=jax.ShapeDtypeStruct((window_tiles, tile_size, col_width), jnp.float32),
        compiler_params=pltpu.CompilerParams(dimension_semantics=("arbitrary",)),
        cost_estimate=pl.CostEstimate(
            flops=flops,
            bytes_accessed=blocks.size * 2 + window_x.size * 2 + window_tiles * tile_size * col_width * 4,
            transcendentals=0,
        ),
    )(rows_local, cols_local, used, blocks, window_x)


def accumulate(window_x, totals, block_tiles, row_ids, col_ids, used_slots, window_start):
    group_total = (used_slots + 7) // 8

    def one_turn(group_index, partial_value):
        first_slot = group_index * 8
        chosen = lax.dynamic_slice_in_dim(block_tiles, first_slot, 8, 0)
        rows_here = lax.dynamic_slice_in_dim(row_ids, first_slot, 8, 0) - window_start
        cols_here = lax.dynamic_slice_in_dim(col_ids, first_slot, 8, 0) - window_start
        alive_mask = (first_slot + jnp.arange(8, dtype=jnp.int32) < used_slots).astype(jnp.float32)
        weight = (jnp.where(rows_here == cols_here, 0.5, 1.0).astype(jnp.float32) * alive_mask)[
            :, None, None
        ]
        direct = (
            jnp.einsum(
                "sab,sbk->sak", chosen, window_x[cols_here], preferred_element_type=jnp.float32
            )
            * weight
        )
        mirror = (
            jnp.einsum(
                "sba,sbk->sak", chosen, window_x[rows_here], preferred_element_type=jnp.float32
            )
            * weight
        )
        return partial_value.at[rows_here].add(direct).at[cols_here].add(mirror)

    return lax.fori_loop(0, group_total, one_turn, totals)


def shards(vectors, blocks, block_row, block_col, block_count):
    dev_rows, col_width = vectors.shape
    tile_size = blocks.shape[1]
    total_rows = dev_rows * lax.axis_size("patch")
    position = lax.axis_index("patch")
    parity = position % 2
    window_start = 2 * (position - 6 - parity)
    column_start = lax.axis_index("vec") * col_width
    used_slots = block_count[0]
    current = vectors
    residual = vectors
    for iteration in range(STEPS):
        rounded = current.astype(jnp.bfloat16)
        pieces = {0: rounded}
        for offset in (7, 6, 5, 4, 3, 2, 1, -1):
            pieces[offset] = shifted(rounded, "patch", offset)
        lower_side = jnp.concatenate([pieces[6 - segment] for segment in range(8)], axis=0)
        upper_side = jnp.concatenate([pieces[7 - segment] for segment in range(8)], axis=0)
        window_x = jnp.where(parity == 0, lower_side, upper_side).reshape(16, tile_size, col_width)
        near_x = jnp.where(
            parity == 0,
            jnp.concatenate([pieces[0], pieces[-1]], axis=0),
            jnp.concatenate([pieces[1], pieces[0]], axis=0),
        ).reshape(4, tile_size, col_width)
        rows_local = block_row - window_start
        cols_local = block_col - window_start
        mirrored = hessian_window(near_x, blocks, rows_local, cols_local, block_count, "mirror", 16)
        directed = hessian_window(window_x, blocks, rows_local, cols_local, block_count, "direct", 16)
        far = mirrored.reshape(8, dev_rows, col_width)
        segments = (mirrored + directed).reshape(8, dev_rows, col_width)
        zero_rows = jnp.zeros((dev_rows, col_width), jnp.float32)
        applied = jnp.where(parity == 0, segments[6], segments[7])
        for offset in (1, -1, -2, -3, -4, -5, -6, -7):
            source = segments if offset >= -1 else far
            lower_seg = source[offset + 6] if 0 <= offset + 6 <= 7 else zero_rows
            upper_seg = source[offset + 7] if 0 <= offset + 7 <= 7 else zero_rows
            outgoing = jnp.where(parity == 0, lower_seg, upper_seg)
            applied = applied + shifted(outgoing, "patch", offset)
        current_all = lax.all_gather(current, "vec", axis=1, tiled=True)
        rayleigh = summed_over_patch(
            jnp.dot(
                current_all.T, applied, precision=exact_mode, preferred_element_type=jnp.float32
            )
            / total_rows,
            0,
        )
        residual = applied - jnp.dot(
            current_all, rayleigh, precision=exact_mode, preferred_element_type=jnp.float32
        )
        update = current - step_rate * residual
        update_all = lax.all_gather(update, "vec", axis=1, tiled=True)
        gram_matrix = summed_over_patch(
            jnp.dot(
                update_all.T, update_all, precision=exact_mode, preferred_element_type=jnp.float32
            )
            / total_rows,
            1,
        )
        factor = jnp.linalg.cholesky(gram_matrix)
        solved = lax.linalg.triangular_solve(
            factor, update_all, left_side=False, lower=True, transpose_a=True
        )
        current = lax.dynamic_slice_in_dim(solved, column_start, col_width, 1)
    return (current, residual)


def solution(mesh):
    in_specs = (P("patch", "vec"), P("patch", None, None), P("patch"), P("patch"), P("patch"))
    out_specs = (P("patch", "vec"), P("patch", "vec"))
    return jax.shard_map(shards, mesh=mesh, in_specs=in_specs, out_specs=out_specs, check_vma=False)
```

```python
import functools

import jax
import jax.numpy as jnp
from jax import lax
from jax.experimental import pallas as pl
from jax.experimental.pallas import tpu as pltpu
from jax.sharding import PartitionSpec as P

STEPS = 2


step_rate = 0.25
exact_mode = lax.Precision.HIGHEST


def shifted(block, axis, distance):
    devices = range(lax.axis_size(axis))
    route = [(i - distance, i) for i in devices if i - distance in devices]
    return lax.ppermute(block, axis, route)


GROUP_ORDERS = (((0, 2), (5, 2), (2, 2), (4, 1)), ((5, 2), (0, 2), (2, 2), (4, 1)))


def digit_groups(size, order=0):
    nbits = size.bit_length() - 1
    return [(low, min(width, nbits - low)) for low, width in GROUP_ORDERS[order] if low < nbits]


def flipped(digit, e, width):
    total = 0
    for bit in range(width):
        total = total + ((digit // (1 << bit) + e // (1 << bit)) % 2) * (1 << bit)
    return total


def exchange_sum(size, x_ref, out_ref, work_ref, recv_ref, final_ref, send_sems, recv_sems):
    me = lax.axis_index("patch")
    groups = digit_groups(size)
    mesh_ids = pl.DeviceIdType.MESH

    def digit_of(low, width):
        return (me // (1 << low)) % (1 << width)

    def partner_of(low, width, e):
        digit = digit_of(low, width)
        return me + (flipped(digit, e, width) - digit) * (1 << low)

    barrier = pltpu.get_barrier_semaphore()
    greeted = 0
    for low, width in groups:
        for e in range(1, 1 << width):
            pl.semaphore_signal(
                barrier, 1, device_id={"patch": partner_of(low, width, e)}, device_id_type=mesh_ids
            )
            greeted += 1
    pl.semaphore_wait(barrier, greeted)
    work_ref[...] = x_ref[...]
    reduce_and_spread = functools.partial(
        exchange_body, me, work_ref, recv_ref, final_ref, send_sems, recv_sems
    )
    core = lax.axis_index("vec")
    for order in range(len(GROUP_ORDERS)):

        @pl.when(core % len(GROUP_ORDERS) == order)
        def _():
            reduce_and_spread(digit_groups(size, order))

    out_ref[...] = final_ref[...]


def exchange_body(me, work_ref, recv_ref, final_ref, send_sems, recv_sems, groups):
    mesh_ids = pl.DeviceIdType.MESH

    def digit_of(low, width):
        return (me // (1 << low)) % (1 << width)

    def partner_of(low, width, e):
        digit = digit_of(low, width)
        return me + (flipped(digit, e, width) - digit) * (1 << low)

    lo = 0
    span = work_ref.shape[0]
    recv_at = 0
    sem = 0
    for low, width in groups:
        ways = 1 << width
        span = span // ways
        digit = digit_of(low, width)
        copies = []
        for e in range(1, ways):
            copy = pltpu.make_async_remote_copy(
                src_ref=work_ref.at[pl.ds(lo + flipped(digit, e, width) * span, span)],
                dst_ref=recv_ref.at[pl.ds(recv_at + (e - 1) * span, span)],
                send_sem=send_sems.at[sem],
                recv_sem=recv_sems.at[sem],
                device_id={"patch": partner_of(low, width, e)},
                device_id_type=mesh_ids,
            )
            copy.start()
            copies.append(copy)
            sem += 1
        for copy in copies:
            copy.wait()
        keep = lo + digit * span
        total = work_ref[pl.ds(keep, span)]
        for e in range(1, ways):
            total = total + recv_ref[pl.ds(recv_at + (e - 1) * span, span)]
        work_ref[pl.ds(keep, span)] = total
        lo = keep
        recv_at += (ways - 1) * span
    final_ref[pl.ds(lo, span)] = work_ref[pl.ds(lo, span)]
    for low, width in reversed(groups):
        ways = 1 << width
        digit = digit_of(low, width)
        copies = []
        for e in range(1, ways):
            copy = pltpu.make_async_remote_copy(
                src_ref=final_ref.at[pl.ds(lo, span)],
                dst_ref=final_ref.at[pl.ds(lo, span)],
                send_sem=send_sems.at[sem],
                recv_sem=recv_sems.at[sem],
                device_id={"patch": partner_of(low, width, e)},
                device_id_type=mesh_ids,
            )
            copy.start()
            copies.append(copy)
            sem += 1
        for copy in copies:
            copy.wait()
        lo = lo - digit * span
        span = span * ways


def summed_over_patch(block, collective):
    size = lax.axis_size("patch")
    rows, cols = block.shape
    flat = block.reshape(size, (rows * cols) // (size * 128), 128)
    steps = 2 * sum((1 << width) - 1 for _, width in digit_groups(size))
    out = pl.pallas_call(
        functools.partial(exchange_sum, size),
        out_shape=jax.ShapeDtypeStruct(flat.shape, flat.dtype),
        in_specs=[pl.BlockSpec(memory_space=pltpu.VMEM)],
        out_specs=pl.BlockSpec(memory_space=pltpu.VMEM),
        scratch_shapes=[
            pltpu.VMEM(flat.shape, flat.dtype),
            pltpu.VMEM(flat.shape, flat.dtype),
            pltpu.VMEM(flat.shape, flat.dtype),
            pltpu.SemaphoreType.DMA((steps,)),
            pltpu.SemaphoreType.DMA((steps,)),
        ],
        compiler_params=pltpu.CompilerParams(collective_id=collective, has_side_effects=True),
    )(flat)
    return out.reshape(rows, cols)


def tile_products(rows_ref, cols_ref, used_ref, tile_ref, x_ref, out_ref):
    slot = pl.program_id(0)

    @pl.when(slot == 0)
    def _():
        out_ref[...] = jnp.zeros_like(out_ref)

    @pl.when(slot < used_ref[0])
    def _():
        row = rows_ref[slot]
        col = cols_ref[slot]
        tile = tile_ref[0]
        weight = jnp.where(row == col, jnp.float32(0.5), jnp.float32(1.0))
        direct = jnp.dot(tile, x_ref[col], preferred_element_type=jnp.float32)
        out_ref[row] += direct * weight
        mirror = lax.dot_general(
            tile, x_ref[row], (((0,), (0,)), ((), ())), preferred_element_type=jnp.float32
        )
        out_ref[col] += mirror * weight


def hessian_window(window_x, blocks, rows_local, cols_local, used):
    slots, tile_size, _ = blocks.shape
    window_tiles, _, col_width = window_x.shape

    def tile_at(slot, rows, cols, used_ref):
        return (jnp.maximum(jnp.minimum(slot, used_ref[0] - 1), 0), 0, 0)

    def whole(slot, rows, cols, used_ref):
        return (0, 0, 0)

    grid_spec = pltpu.PrefetchScalarGridSpec(
        num_scalar_prefetch=3,
        grid=(slots,),
        in_specs=[
            pl.BlockSpec((1, tile_size, tile_size), tile_at),
            pl.BlockSpec((window_tiles, tile_size, col_width), whole),
        ],
        out_specs=pl.BlockSpec((window_tiles, tile_size, col_width), whole),
    )
    flops = 4 * slots * tile_size * tile_size * col_width
    return pl.pallas_call(
        tile_products,
        grid_spec=grid_spec,
        out_shape=jax.ShapeDtypeStruct((window_tiles, tile_size, col_width), jnp.float32),
        compiler_params=pltpu.CompilerParams(dimension_semantics=("arbitrary",)),
        cost_estimate=pl.CostEstimate(
            flops=flops,
            bytes_accessed=blocks.size * 2 + window_x.size * 2 + window_tiles * tile_size * col_width * 4,
            transcendentals=0,
        ),
    )(rows_local, cols_local, used, blocks, window_x)


def accumulate(window_x, totals, block_tiles, row_ids, col_ids, used_slots, window_start):
    group_total = (used_slots + 7) // 8

    def one_turn(group_index, partial_value):
        first_slot = group_index * 8
        chosen = lax.dynamic_slice_in_dim(block_tiles, first_slot, 8, 0)
        rows_here = lax.dynamic_slice_in_dim(row_ids, first_slot, 8, 0) - window_start
        cols_here = lax.dynamic_slice_in_dim(col_ids, first_slot, 8, 0) - window_start
        alive_mask = (first_slot + jnp.arange(8, dtype=jnp.int32) < used_slots).astype(jnp.float32)
        weight = (jnp.where(rows_here == cols_here, 0.5, 1.0).astype(jnp.float32) * alive_mask)[
            :, None, None
        ]
        direct = (
            jnp.einsum(
                "sab,sbk->sak", chosen, window_x[cols_here], preferred_element_type=jnp.float32
            )
            * weight
        )
        mirror = (
            jnp.einsum(
                "sba,sbk->sak", chosen, window_x[rows_here], preferred_element_type=jnp.float32
            )
            * weight
        )
        return partial_value.at[rows_here].add(direct).at[cols_here].add(mirror)

    return lax.fori_loop(0, group_total, one_turn, totals)


def shards(vectors, blocks, block_row, block_col, block_count):
    dev_rows, col_width = vectors.shape
    tile_size = blocks.shape[1]
    total_rows = dev_rows * lax.axis_size("patch")
    position = lax.axis_index("patch")
    parity = position % 2
    window_start = 2 * (position - 6 - parity)
    column_start = lax.axis_index("vec") * col_width
    used_slots = block_count[0]
    current = vectors
    residual = vectors
    for iteration in range(STEPS):
        rounded = current.astype(jnp.bfloat16)
        pieces = {0: rounded}
        for offset in (7, 6, 5, 4, 3, 2, 1, -1):
            pieces[offset] = shifted(rounded, "patch", offset)
        lower_side = jnp.concatenate([pieces[6 - segment] for segment in range(8)], axis=0)
        upper_side = jnp.concatenate([pieces[7 - segment] for segment in range(8)], axis=0)
        window_x = jnp.where(parity == 0, lower_side, upper_side).reshape(16, tile_size, col_width)
        totals = hessian_window(
            window_x, blocks, block_row - window_start, block_col - window_start, block_count
        )
        segments = totals.reshape(8, dev_rows, col_width)
        zero_rows = jnp.zeros((dev_rows, col_width), jnp.float32)
        applied = jnp.where(parity == 0, segments[6], segments[7])
        for offset in (1, -1, -2, -3, -4, -5, -6, -7):
            lower_seg = segments[offset + 6] if 0 <= offset + 6 <= 7 else zero_rows
            upper_seg = segments[offset + 7] if 0 <= offset + 7 <= 7 else zero_rows
            outgoing = jnp.where(parity == 0, lower_seg, upper_seg)
            applied = applied + shifted(outgoing, "patch", offset)
        current_all = lax.all_gather(current, "vec", axis=1, tiled=True)
        rayleigh = summed_over_patch(
            jnp.dot(
                current_all.T, applied, precision=exact_mode, preferred_element_type=jnp.float32
            )
            / total_rows,
            0,
        )
        residual = applied - jnp.dot(
            current_all, rayleigh, precision=exact_mode, preferred_element_type=jnp.float32
        )
        update = current - step_rate * residual
        update_all = lax.all_gather(update, "vec", axis=1, tiled=True)
        gram_matrix = summed_over_patch(
            jnp.dot(
                update_all.T, update_all, precision=exact_mode, preferred_element_type=jnp.float32
            )
            / total_rows,
            1,
        )
        factor = jnp.linalg.cholesky(gram_matrix)
        solved = lax.linalg.triangular_solve(
            factor, update_all, left_side=False, lower=True, transpose_a=True
        )
        current = lax.dynamic_slice_in_dim(solved, column_start, col_width, 1)
    return (current, residual)


def solution(mesh):
    in_specs = (P("patch", "vec"), P("patch", None, None), P("patch"), P("patch"), P("patch"))
    out_specs = (P("patch", "vec"), P("patch", "vec"))
    return jax.shard_map(shards, mesh=mesh, in_specs=in_specs, out_specs=out_specs, check_vma=False)
```

```python
import functools

import jax
import jax.numpy as jnp
from jax import lax
from jax.experimental import pallas as pl
from jax.experimental.pallas import tpu as pltpu
from jax.sharding import PartitionSpec as P

STEPS = 2


step_rate = 0.25
exact_mode = lax.Precision.HIGHEST


def shifted(block, axis, distance):
    devices = range(lax.axis_size(axis))
    route = [(i - distance, i) for i in devices if i - distance in devices]
    return lax.ppermute(block, axis, route)


GROUP_ORDERS = (((0, 2), (5, 2), (2, 2), (4, 1)), ((5, 2), (0, 2), (2, 2), (4, 1)))


def digit_groups(size, order=0):
    nbits = size.bit_length() - 1
    return [(low, min(width, nbits - low)) for low, width in GROUP_ORDERS[order] if low < nbits]


def flipped(digit, e, width):
    total = 0
    for bit in range(width):
        total = total + ((digit // (1 << bit) + e // (1 << bit)) % 2) * (1 << bit)
    return total


def exchange_sum(size, x_ref, out_ref, work_ref, recv_ref, final_ref, send_sems, recv_sems):
    me = lax.axis_index("patch")
    groups = digit_groups(size)
    mesh_ids = pl.DeviceIdType.MESH

    def digit_of(low, width):
        return (me // (1 << low)) % (1 << width)

    def partner_of(low, width, e):
        digit = digit_of(low, width)
        return me + (flipped(digit, e, width) - digit) * (1 << low)

    barrier = pltpu.get_barrier_semaphore()
    greeted = 0
    for low, width in groups:
        for e in range(1, 1 << width):
            pl.semaphore_signal(
                barrier, 1, device_id={"patch": partner_of(low, width, e)}, device_id_type=mesh_ids
            )
            greeted += 1
    pl.semaphore_wait(barrier, greeted)
    work_ref[...] = x_ref[...]
    reduce_and_spread = functools.partial(
        exchange_body, me, work_ref, recv_ref, final_ref, send_sems, recv_sems
    )
    core = lax.axis_index("vec")
    for order in range(len(GROUP_ORDERS)):

        @pl.when(core % len(GROUP_ORDERS) == order)
        def _():
            reduce_and_spread(digit_groups(size, order))

    out_ref[...] = final_ref[...]


def exchange_body(me, work_ref, recv_ref, final_ref, send_sems, recv_sems, groups):
    mesh_ids = pl.DeviceIdType.MESH

    def digit_of(low, width):
        return (me // (1 << low)) % (1 << width)

    def partner_of(low, width, e):
        digit = digit_of(low, width)
        return me + (flipped(digit, e, width) - digit) * (1 << low)

    lo = 0
    span = work_ref.shape[0]
    recv_at = 0
    sem = 0
    for low, width in groups:
        ways = 1 << width
        span = span // ways
        digit = digit_of(low, width)
        copies = []
        for e in range(1, ways):
            copy = pltpu.make_async_remote_copy(
                src_ref=work_ref.at[pl.ds(lo + flipped(digit, e, width) * span, span)],
                dst_ref=recv_ref.at[pl.ds(recv_at + (e - 1) * span, span)],
                send_sem=send_sems.at[sem],
                recv_sem=recv_sems.at[sem],
                device_id={"patch": partner_of(low, width, e)},
                device_id_type=mesh_ids,
            )
            copy.start()
            copies.append(copy)
            sem += 1
        for copy in copies:
            copy.wait()
        keep = lo + digit * span
        total = work_ref[pl.ds(keep, span)]
        for e in range(1, ways):
            total = total + recv_ref[pl.ds(recv_at + (e - 1) * span, span)]
        work_ref[pl.ds(keep, span)] = total
        lo = keep
        recv_at += (ways - 1) * span
    final_ref[pl.ds(lo, span)] = work_ref[pl.ds(lo, span)]
    for low, width in reversed(groups):
        ways = 1 << width
        digit = digit_of(low, width)
        copies = []
        for e in range(1, ways):
            copy = pltpu.make_async_remote_copy(
                src_ref=final_ref.at[pl.ds(lo, span)],
                dst_ref=final_ref.at[pl.ds(lo, span)],
                send_sem=send_sems.at[sem],
                recv_sem=recv_sems.at[sem],
                device_id={"patch": partner_of(low, width, e)},
                device_id_type=mesh_ids,
            )
            copy.start()
            copies.append(copy)
            sem += 1
        for copy in copies:
            copy.wait()
        lo = lo - digit * span
        span = span * ways


def summed_over_patch(block, collective):
    size = lax.axis_size("patch")
    rows, cols = block.shape
    flat = block.reshape(size, (rows * cols) // (size * 128), 128)
    steps = 2 * sum((1 << width) - 1 for _, width in digit_groups(size))
    out = pl.pallas_call(
        functools.partial(exchange_sum, size),
        out_shape=jax.ShapeDtypeStruct(flat.shape, flat.dtype),
        in_specs=[pl.BlockSpec(memory_space=pltpu.VMEM)],
        out_specs=pl.BlockSpec(memory_space=pltpu.VMEM),
        scratch_shapes=[
            pltpu.VMEM(flat.shape, flat.dtype),
            pltpu.VMEM(flat.shape, flat.dtype),
            pltpu.VMEM(flat.shape, flat.dtype),
            pltpu.SemaphoreType.DMA((steps,)),
            pltpu.SemaphoreType.DMA((steps,)),
        ],
        compiler_params=pltpu.CompilerParams(collective_id=collective, has_side_effects=True),
    )(flat)
    return out.reshape(rows, cols)


def swap_halves(x_ref, out_ref, recv_ref, send_sem, recv_sem):
    core = lax.axis_index("vec")
    sibling = 1 - core
    mesh_ids = pl.DeviceIdType.MESH
    barrier = pltpu.get_barrier_semaphore()
    pl.semaphore_signal(barrier, 1, device_id={"vec": sibling}, device_id_type=mesh_ids)
    pl.semaphore_wait(barrier, 1)
    copy = pltpu.make_async_remote_copy(
        src_ref=x_ref,
        dst_ref=recv_ref,
        send_sem=send_sem,
        recv_sem=recv_sem,
        device_id={"vec": sibling},
        device_id_type=mesh_ids,
    )
    copy.start()
    out_ref[core] = x_ref[...]
    copy.wait()
    out_ref[sibling] = recv_ref[...]


def gathered_over_vec(block):
    halves = pl.pallas_call(
        swap_halves,
        out_shape=jax.ShapeDtypeStruct((2, *block.shape), block.dtype),
        in_specs=[pl.BlockSpec(memory_space=pltpu.VMEM)],
        out_specs=pl.BlockSpec(memory_space=pltpu.VMEM),
        scratch_shapes=[
            pltpu.VMEM(block.shape, block.dtype),
            pltpu.SemaphoreType.DMA(()),
            pltpu.SemaphoreType.DMA(()),
        ],
        compiler_params=pltpu.CompilerParams(collective_id=2, has_side_effects=True),
    )(block)
    return jnp.concatenate([halves[0], halves[1]], axis=1)


def tile_products(rows_ref, cols_ref, used_ref, tile_ref, x_ref, out_ref):
    slot = pl.program_id(0)

    @pl.when(slot == 0)
    def _():
        out_ref[...] = jnp.zeros_like(out_ref)

    @pl.when(slot < used_ref[0])
    def _():
        row = rows_ref[slot]
        col = cols_ref[slot]
        tile = tile_ref[0]
        weight = jnp.where(row == col, jnp.float32(0.5), jnp.float32(1.0))
        direct = jnp.dot(tile, x_ref[col], preferred_element_type=jnp.float32)
        out_ref[row] += direct * weight
        mirror = lax.dot_general(
            tile, x_ref[row], (((0,), (0,)), ((), ())), preferred_element_type=jnp.float32
        )
        out_ref[col] += mirror * weight


def hessian_window(window_x, blocks, rows_local, cols_local, used):
    slots, tile_size, _ = blocks.shape
    window_tiles, _, col_width = window_x.shape

    def tile_at(slot, rows, cols, used_ref):
        return (jnp.maximum(jnp.minimum(slot, used_ref[0] - 1), 0), 0, 0)

    def whole(slot, rows, cols, used_ref):
        return (0, 0, 0)

    grid_spec = pltpu.PrefetchScalarGridSpec(
        num_scalar_prefetch=3,
        grid=(slots,),
        in_specs=[
            pl.BlockSpec((1, tile_size, tile_size), tile_at),
            pl.BlockSpec((window_tiles, tile_size, col_width), whole),
        ],
        out_specs=pl.BlockSpec((window_tiles, tile_size, col_width), whole),
    )
    flops = 4 * slots * tile_size * tile_size * col_width
    return pl.pallas_call(
        tile_products,
        grid_spec=grid_spec,
        out_shape=jax.ShapeDtypeStruct((window_tiles, tile_size, col_width), jnp.float32),
        compiler_params=pltpu.CompilerParams(dimension_semantics=("arbitrary",)),
        cost_estimate=pl.CostEstimate(
            flops=flops,
            bytes_accessed=blocks.size * 2 + window_x.size * 2 + window_tiles * tile_size * col_width * 4,
            transcendentals=0,
        ),
    )(rows_local, cols_local, used, blocks, window_x)


def accumulate(window_x, totals, block_tiles, row_ids, col_ids, used_slots, window_start):
    group_total = (used_slots + 7) // 8

    def one_turn(group_index, partial_value):
        first_slot = group_index * 8
        chosen = lax.dynamic_slice_in_dim(block_tiles, first_slot, 8, 0)
        rows_here = lax.dynamic_slice_in_dim(row_ids, first_slot, 8, 0) - window_start
        cols_here = lax.dynamic_slice_in_dim(col_ids, first_slot, 8, 0) - window_start
        alive_mask = (first_slot + jnp.arange(8, dtype=jnp.int32) < used_slots).astype(jnp.float32)
        weight = (jnp.where(rows_here == cols_here, 0.5, 1.0).astype(jnp.float32) * alive_mask)[
            :, None, None
        ]
        direct = (
            jnp.einsum(
                "sab,sbk->sak", chosen, window_x[cols_here], preferred_element_type=jnp.float32
            )
            * weight
        )
        mirror = (
            jnp.einsum(
                "sba,sbk->sak", chosen, window_x[rows_here], preferred_element_type=jnp.float32
            )
            * weight
        )
        return partial_value.at[rows_here].add(direct).at[cols_here].add(mirror)

    return lax.fori_loop(0, group_total, one_turn, totals)


def shards(vectors, blocks, block_row, block_col, block_count):
    dev_rows, col_width = vectors.shape
    tile_size = blocks.shape[1]
    total_rows = dev_rows * lax.axis_size("patch")
    position = lax.axis_index("patch")
    parity = position % 2
    window_start = 2 * (position - 6 - parity)
    column_start = lax.axis_index("vec") * col_width
    used_slots = block_count[0]
    current = vectors
    residual = vectors
    for iteration in range(STEPS):
        rounded = current.astype(jnp.bfloat16)
        pieces = {0: rounded}
        for offset in (7, 6, 5, 4, 3, 2, 1, -1):
            pieces[offset] = shifted(rounded, "patch", offset)
        lower_side = jnp.concatenate([pieces[6 - segment] for segment in range(8)], axis=0)
        upper_side = jnp.concatenate([pieces[7 - segment] for segment in range(8)], axis=0)
        window_x = jnp.where(parity == 0, lower_side, upper_side).reshape(16, tile_size, col_width)
        totals = hessian_window(
            window_x, blocks, block_row - window_start, block_col - window_start, block_count
        )
        segments = totals.reshape(8, dev_rows, col_width)
        zero_rows = jnp.zeros((dev_rows, col_width), jnp.float32)
        applied = jnp.where(parity == 0, segments[6], segments[7])
        for offset in (1, -1, -2, -3, -4, -5, -6, -7):
            lower_seg = segments[offset + 6] if 0 <= offset + 6 <= 7 else zero_rows
            upper_seg = segments[offset + 7] if 0 <= offset + 7 <= 7 else zero_rows
            outgoing = jnp.where(parity == 0, lower_seg, upper_seg)
            applied = applied + shifted(outgoing, "patch", offset)
        current_all = lax.all_gather(current, "vec", axis=1, tiled=True)
        rayleigh = summed_over_patch(
            jnp.dot(
                current_all.T, applied, precision=exact_mode, preferred_element_type=jnp.float32
            )
            / total_rows,
            0,
        )
        residual = applied - jnp.dot(
            current_all, rayleigh, precision=exact_mode, preferred_element_type=jnp.float32
        )
        update = current - step_rate * residual
        update_all = gathered_over_vec(update)
        gram_matrix = summed_over_patch(
            jnp.dot(
                update_all.T, update_all, precision=exact_mode, preferred_element_type=jnp.float32
            )
            / total_rows,
            1,
        )
        factor = jnp.linalg.cholesky(gram_matrix)
        solved = lax.linalg.triangular_solve(
            factor, update_all, left_side=False, lower=True, transpose_a=True
        )
        current = lax.dynamic_slice_in_dim(solved, column_start, col_width, 1)
    return (current, residual)


def solution(mesh):
    in_specs = (P("patch", "vec"), P("patch", None, None), P("patch"), P("patch"), P("patch"))
    out_specs = (P("patch", "vec"), P("patch", "vec"))
    return jax.shard_map(shards, mesh=mesh, in_specs=in_specs, out_specs=out_specs, check_vma=False)
```

```python
import functools

import jax
import jax.numpy as jnp
from jax import lax
from jax.experimental import pallas as pl
from jax.experimental.pallas import tpu as pltpu
from jax.sharding import PartitionSpec as P

STEPS = 2


step_rate = 0.25
exact_mode = lax.Precision.HIGHEST


def shifted(block, axis, distance):
    devices = range(lax.axis_size(axis))
    route = [(i - distance, i) for i in devices if i - distance in devices]
    return lax.ppermute(block, axis, route)


GROUP_ORDERS = (((0, 2), (5, 2), (2, 2), (4, 1)), ((5, 2), (0, 2), (2, 2), (4, 1)))


def digit_groups(size, order=0):
    nbits = size.bit_length() - 1
    return [(low, min(width, nbits - low)) for low, width in GROUP_ORDERS[order] if low < nbits]


def flipped(digit, e, width):
    total = 0
    for bit in range(width):
        total = total + ((digit // (1 << bit) + e // (1 << bit)) % 2) * (1 << bit)
    return total


def exchange_sum(size, x_ref, out_ref, work_ref, recv_ref, final_ref, send_sems, recv_sems):
    me = lax.axis_index("patch")
    groups = digit_groups(size)
    mesh_ids = pl.DeviceIdType.MESH

    def digit_of(low, width):
        return (me // (1 << low)) % (1 << width)

    def partner_of(low, width, e):
        digit = digit_of(low, width)
        return me + (flipped(digit, e, width) - digit) * (1 << low)

    barrier = pltpu.get_barrier_semaphore()
    greeted = 0
    for low, width in groups:
        for e in range(1, 1 << width):
            pl.semaphore_signal(
                barrier, 1, device_id={"patch": partner_of(low, width, e)}, device_id_type=mesh_ids
            )
            greeted += 1
    pl.semaphore_wait(barrier, greeted)
    work_ref[...] = x_ref[...]
    reduce_and_spread = functools.partial(
        exchange_body, me, work_ref, recv_ref, final_ref, send_sems, recv_sems
    )
    core = lax.axis_index("vec")
    for order in range(len(GROUP_ORDERS)):

        @pl.when(core % len(GROUP_ORDERS) == order)
        def _():
            reduce_and_spread(digit_groups(size, order))

    out_ref[...] = final_ref[...]


def exchange_body(me, work_ref, recv_ref, final_ref, send_sems, recv_sems, groups):
    mesh_ids = pl.DeviceIdType.MESH

    def digit_of(low, width):
        return (me // (1 << low)) % (1 << width)

    def partner_of(low, width, e):
        digit = digit_of(low, width)
        return me + (flipped(digit, e, width) - digit) * (1 << low)

    lo = 0
    span = work_ref.shape[0]
    recv_at = 0
    sem = 0
    for low, width in groups:
        ways = 1 << width
        span = span // ways
        digit = digit_of(low, width)
        copies = []
        for e in range(1, ways):
            copy = pltpu.make_async_remote_copy(
                src_ref=work_ref.at[pl.ds(lo + flipped(digit, e, width) * span, span)],
                dst_ref=recv_ref.at[pl.ds(recv_at + (e - 1) * span, span)],
                send_sem=send_sems.at[sem],
                recv_sem=recv_sems.at[sem],
                device_id={"patch": partner_of(low, width, e)},
                device_id_type=mesh_ids,
            )
            copy.start()
            copies.append(copy)
            sem += 1
        for copy in copies:
            copy.wait()
        keep = lo + digit * span
        total = work_ref[pl.ds(keep, span)]
        for e in range(1, ways):
            total = total + recv_ref[pl.ds(recv_at + (e - 1) * span, span)]
        work_ref[pl.ds(keep, span)] = total
        lo = keep
        recv_at += (ways - 1) * span
    final_ref[pl.ds(lo, span)] = work_ref[pl.ds(lo, span)]
    for low, width in reversed(groups):
        ways = 1 << width
        digit = digit_of(low, width)
        copies = []
        for e in range(1, ways):
            copy = pltpu.make_async_remote_copy(
                src_ref=final_ref.at[pl.ds(lo, span)],
                dst_ref=final_ref.at[pl.ds(lo, span)],
                send_sem=send_sems.at[sem],
                recv_sem=recv_sems.at[sem],
                device_id={"patch": partner_of(low, width, e)},
                device_id_type=mesh_ids,
            )
            copy.start()
            copies.append(copy)
            sem += 1
        for copy in copies:
            copy.wait()
        lo = lo - digit * span
        span = span * ways


def summed_over_patch(block, collective):
    size = lax.axis_size("patch")
    rows, cols = block.shape
    flat = block.reshape(size, (rows * cols) // (size * 128), 128)
    steps = 2 * sum((1 << width) - 1 for _, width in digit_groups(size))
    out = pl.pallas_call(
        functools.partial(exchange_sum, size),
        out_shape=jax.ShapeDtypeStruct(flat.shape, flat.dtype),
        in_specs=[pl.BlockSpec(memory_space=pltpu.VMEM)],
        out_specs=pl.BlockSpec(memory_space=pltpu.VMEM),
        scratch_shapes=[
            pltpu.VMEM(flat.shape, flat.dtype),
            pltpu.VMEM(flat.shape, flat.dtype),
            pltpu.VMEM(flat.shape, flat.dtype),
            pltpu.SemaphoreType.DMA((steps,)),
            pltpu.SemaphoreType.DMA((steps,)),
        ],
        compiler_params=pltpu.CompilerParams(collective_id=collective, has_side_effects=True),
    )(flat)
    return out.reshape(rows, cols)


def swap_halves(x_ref, out_ref, recv_ref, send_sem, recv_sem):
    core = lax.axis_index("vec")
    sibling = 1 - core
    mesh_ids = pl.DeviceIdType.MESH
    barrier = pltpu.get_barrier_semaphore()
    pl.semaphore_signal(barrier, 1, device_id={"vec": sibling}, device_id_type=mesh_ids)
    pl.semaphore_wait(barrier, 1)
    copy = pltpu.make_async_remote_copy(
        src_ref=x_ref,
        dst_ref=recv_ref,
        send_sem=send_sem,
        recv_sem=recv_sem,
        device_id={"vec": sibling},
        device_id_type=mesh_ids,
    )
    copy.start()
    out_ref[core] = x_ref[...]
    copy.wait()
    out_ref[sibling] = recv_ref[...]


def gathered_over_vec(block):
    halves = pl.pallas_call(
        swap_halves,
        out_shape=jax.ShapeDtypeStruct((2, *block.shape), block.dtype),
        in_specs=[pl.BlockSpec(memory_space=pltpu.VMEM)],
        out_specs=pl.BlockSpec(memory_space=pltpu.VMEM),
        scratch_shapes=[
            pltpu.VMEM(block.shape, block.dtype),
            pltpu.SemaphoreType.DMA(()),
            pltpu.SemaphoreType.DMA(()),
        ],
        compiler_params=pltpu.CompilerParams(collective_id=2, has_side_effects=True),
    )(block)
    return jnp.concatenate([halves[0], halves[1]], axis=1)


def tile_products(rows_ref, cols_ref, used_ref, tile_ref, x_ref, out_ref):
    slot = pl.program_id(0)

    @pl.when(slot == 0)
    def _():
        out_ref[...] = jnp.zeros_like(out_ref)

    @pl.when(slot < used_ref[0])
    def _():
        row = rows_ref[slot]
        col = cols_ref[slot]
        tile = tile_ref[0]
        weight = jnp.where(row == col, jnp.float32(0.5), jnp.float32(1.0))
        direct = jnp.dot(tile, x_ref[col], preferred_element_type=jnp.float32)
        out_ref[row] += direct * weight
        mirror = lax.dot_general(
            tile, x_ref[row], (((0,), (0,)), ((), ())), preferred_element_type=jnp.float32
        )
        out_ref[col] += mirror * weight


def hessian_window(window_x, blocks, rows_local, cols_local, used):
    slots, tile_size, _ = blocks.shape
    window_tiles, _, col_width = window_x.shape

    def tile_at(slot, rows, cols, used_ref):
        return (jnp.maximum(jnp.minimum(slot, used_ref[0] - 1), 0), 0, 0)

    def whole(slot, rows, cols, used_ref):
        return (0, 0, 0)

    grid_spec = pltpu.PrefetchScalarGridSpec(
        num_scalar_prefetch=3,
        grid=(slots,),
        in_specs=[
            pl.BlockSpec((1, tile_size, tile_size), tile_at),
            pl.BlockSpec((window_tiles, tile_size, col_width), whole),
        ],
        out_specs=pl.BlockSpec((window_tiles, tile_size, col_width), whole),
    )
    flops = 4 * slots * tile_size * tile_size * col_width
    return pl.pallas_call(
        tile_products,
        grid_spec=grid_spec,
        out_shape=jax.ShapeDtypeStruct((window_tiles, tile_size, col_width), jnp.float32),
        compiler_params=pltpu.CompilerParams(dimension_semantics=("arbitrary",)),
        cost_estimate=pl.CostEstimate(
            flops=flops,
            bytes_accessed=blocks.size * 2 + window_x.size * 2 + window_tiles * tile_size * col_width * 4,
            transcendentals=0,
        ),
    )(rows_local, cols_local, used, blocks, window_x)


def accumulate(window_x, totals, block_tiles, row_ids, col_ids, used_slots, window_start):
    group_total = (used_slots + 7) // 8

    def one_turn(group_index, partial_value):
        first_slot = group_index * 8
        chosen = lax.dynamic_slice_in_dim(block_tiles, first_slot, 8, 0)
        rows_here = lax.dynamic_slice_in_dim(row_ids, first_slot, 8, 0) - window_start
        cols_here = lax.dynamic_slice_in_dim(col_ids, first_slot, 8, 0) - window_start
        alive_mask = (first_slot + jnp.arange(8, dtype=jnp.int32) < used_slots).astype(jnp.float32)
        weight = (jnp.where(rows_here == cols_here, 0.5, 1.0).astype(jnp.float32) * alive_mask)[
            :, None, None
        ]
        direct = (
            jnp.einsum(
                "sab,sbk->sak", chosen, window_x[cols_here], preferred_element_type=jnp.float32
            )
            * weight
        )
        mirror = (
            jnp.einsum(
                "sba,sbk->sak", chosen, window_x[rows_here], preferred_element_type=jnp.float32
            )
            * weight
        )
        return partial_value.at[rows_here].add(direct).at[cols_here].add(mirror)

    return lax.fori_loop(0, group_total, one_turn, totals)


def shards(vectors, blocks, block_row, block_col, block_count):
    dev_rows, col_width = vectors.shape
    tile_size = blocks.shape[1]
    total_rows = dev_rows * lax.axis_size("patch")
    position = lax.axis_index("patch")
    parity = position % 2
    window_start = 2 * (position - 6 - parity)
    column_start = lax.axis_index("vec") * col_width
    used_slots = block_count[0]
    current = vectors
    residual = vectors
    for iteration in range(STEPS):
        rounded = current.astype(jnp.bfloat16)
        pieces = {0: rounded}
        for offset in (7, 6, 5, 4, 3, 2, 1, -1):
            pieces[offset] = shifted(rounded, "patch", offset)
        lower_side = jnp.concatenate([pieces[6 - segment] for segment in range(8)], axis=0)
        upper_side = jnp.concatenate([pieces[7 - segment] for segment in range(8)], axis=0)
        window_x = jnp.where(parity == 0, lower_side, upper_side).reshape(16, tile_size, col_width)
        totals = hessian_window(
            window_x, blocks, block_row - window_start, block_col - window_start, block_count
        )
        segments = totals.reshape(8, dev_rows, col_width)
        zero_rows = jnp.zeros((dev_rows, col_width), jnp.float32)
        applied = jnp.where(parity == 0, segments[6], segments[7])
        for offset in (1, -1, -2, -3, -4, -5, -6, -7):
            lower_seg = segments[offset + 6] if 0 <= offset + 6 <= 7 else zero_rows
            upper_seg = segments[offset + 7] if 0 <= offset + 7 <= 7 else zero_rows
            outgoing = jnp.where(parity == 0, lower_seg, upper_seg)
            applied = applied + shifted(outgoing, "patch", offset)
        current_all = gathered_over_vec(current)
        rayleigh = summed_over_patch(
            jnp.dot(
                current_all.T, applied, precision=exact_mode, preferred_element_type=jnp.float32
            )
            / total_rows,
            0,
        )
        residual = applied - jnp.dot(
            current_all, rayleigh, precision=exact_mode, preferred_element_type=jnp.float32
        )
        update = current - step_rate * residual
        update_all = gathered_over_vec(update)
        gram_matrix = summed_over_patch(
            jnp.dot(
                update_all.T, update_all, precision=exact_mode, preferred_element_type=jnp.float32
            )
            / total_rows,
            1,
        )
        factor = jnp.linalg.cholesky(gram_matrix)
        solved = lax.linalg.triangular_solve(
            factor, update_all, left_side=False, lower=True, transpose_a=True
        )
        current = lax.dynamic_slice_in_dim(solved, column_start, col_width, 1)
    return (current, residual)


def solution(mesh):
    in_specs = (P("patch", "vec"), P("patch", None, None), P("patch"), P("patch"), P("patch"))
    out_specs = (P("patch", "vec"), P("patch", "vec"))
    return jax.shard_map(shards, mesh=mesh, in_specs=in_specs, out_specs=out_specs, check_vma=False)
```

```python
import functools

import jax
import jax.numpy as jnp
from jax import lax
from jax.experimental import pallas as pl
from jax.experimental.pallas import tpu as pltpu
from jax.sharding import PartitionSpec as P

STEPS = 2


step_rate = 0.25
exact_mode = lax.Precision.HIGHEST


def shifted(block, axis, distance):
    devices = range(lax.axis_size(axis))
    route = [(i - distance, i) for i in devices if i - distance in devices]
    return lax.ppermute(block, axis, route)


GROUP_ORDERS = (((0, 2), (5, 2), (2, 2), (4, 1)), ((5, 2), (0, 2), (2, 2), (4, 1)))


def digit_groups(size, order=0):
    nbits = size.bit_length() - 1
    return [(low, min(width, nbits - low)) for low, width in GROUP_ORDERS[order] if low < nbits]


def flipped(digit, e, width):
    total = 0
    for bit in range(width):
        total = total + ((digit // (1 << bit) + e // (1 << bit)) % 2) * (1 << bit)
    return total


def exchange_sum(size, x_ref, out_ref, work_ref, recv_ref, final_ref, send_sems, recv_sems):
    me = lax.axis_index("patch")
    groups = digit_groups(size)
    mesh_ids = pl.DeviceIdType.MESH

    def digit_of(low, width):
        return (me // (1 << low)) % (1 << width)

    def partner_of(low, width, e):
        digit = digit_of(low, width)
        return me + (flipped(digit, e, width) - digit) * (1 << low)

    barrier = pltpu.get_barrier_semaphore()
    greeted = 0
    for low, width in groups:
        for e in range(1, 1 << width):
            pl.semaphore_signal(
                barrier, 1, device_id={"patch": partner_of(low, width, e)}, device_id_type=mesh_ids
            )
            greeted += 1
    pl.semaphore_wait(barrier, greeted)
    work_ref[...] = x_ref[...]
    reduce_and_spread = functools.partial(
        exchange_body, me, work_ref, recv_ref, final_ref, send_sems, recv_sems
    )
    core = lax.axis_index("vec")
    for order in range(len(GROUP_ORDERS)):

        @pl.when(core % len(GROUP_ORDERS) == order)
        def _():
            reduce_and_spread(digit_groups(size, order))

    out_ref[...] = final_ref[...]


def exchange_body(me, work_ref, recv_ref, final_ref, send_sems, recv_sems, groups):
    mesh_ids = pl.DeviceIdType.MESH

    def digit_of(low, width):
        return (me // (1 << low)) % (1 << width)

    def partner_of(low, width, e):
        digit = digit_of(low, width)
        return me + (flipped(digit, e, width) - digit) * (1 << low)

    lo = 0
    span = work_ref.shape[0]
    recv_at = 0
    sem = 0
    for low, width in groups:
        ways = 1 << width
        span = span // ways
        digit = digit_of(low, width)
        copies = []
        for e in range(1, ways):
            copy = pltpu.make_async_remote_copy(
                src_ref=work_ref.at[pl.ds(lo + flipped(digit, e, width) * span, span)],
                dst_ref=recv_ref.at[pl.ds(recv_at + (e - 1) * span, span)],
                send_sem=send_sems.at[sem],
                recv_sem=recv_sems.at[sem],
                device_id={"patch": partner_of(low, width, e)},
                device_id_type=mesh_ids,
            )
            copy.start()
            copies.append(copy)
            sem += 1
        for copy in copies:
            copy.wait()
        keep = lo + digit * span
        total = work_ref[pl.ds(keep, span)]
        for e in range(1, ways):
            total = total + recv_ref[pl.ds(recv_at + (e - 1) * span, span)]
        work_ref[pl.ds(keep, span)] = total
        lo = keep
        recv_at += (ways - 1) * span
    final_ref[pl.ds(lo, span)] = work_ref[pl.ds(lo, span)]
    for low, width in reversed(groups):
        ways = 1 << width
        digit = digit_of(low, width)
        copies = []
        for e in range(1, ways):
            copy = pltpu.make_async_remote_copy(
                src_ref=final_ref.at[pl.ds(lo, span)],
                dst_ref=final_ref.at[pl.ds(lo, span)],
                send_sem=send_sems.at[sem],
                recv_sem=recv_sems.at[sem],
                device_id={"patch": partner_of(low, width, e)},
                device_id_type=mesh_ids,
            )
            copy.start()
            copies.append(copy)
            sem += 1
        for copy in copies:
            copy.wait()
        lo = lo - digit * span
        span = span * ways


def summed_over_patch(block, collective):
    size = lax.axis_size("patch")
    rows, cols = block.shape
    flat = block.reshape(size, (rows * cols) // (size * 128), 128)
    steps = 2 * sum((1 << width) - 1 for _, width in digit_groups(size))
    out = pl.pallas_call(
        functools.partial(exchange_sum, size),
        out_shape=jax.ShapeDtypeStruct(flat.shape, flat.dtype),
        in_specs=[pl.BlockSpec(memory_space=pltpu.VMEM)],
        out_specs=pl.BlockSpec(memory_space=pltpu.VMEM),
        scratch_shapes=[
            pltpu.VMEM(flat.shape, flat.dtype),
            pltpu.VMEM(flat.shape, flat.dtype),
            pltpu.VMEM(flat.shape, flat.dtype),
            pltpu.SemaphoreType.DMA((steps,)),
            pltpu.SemaphoreType.DMA((steps,)),
        ],
        compiler_params=pltpu.CompilerParams(collective_id=collective, has_side_effects=True),
    )(flat)
    return out.reshape(rows, cols)


def swap_halves(x_ref, out_ref, recv_ref, send_sem, recv_sem):
    core = lax.axis_index("vec")
    sibling = 1 - core
    mesh_ids = pl.DeviceIdType.MESH
    barrier = pltpu.get_barrier_semaphore()
    pl.semaphore_signal(barrier, 1, device_id={"vec": sibling}, device_id_type=mesh_ids)
    pl.semaphore_wait(barrier, 1)
    copy = pltpu.make_async_remote_copy(
        src_ref=x_ref,
        dst_ref=recv_ref,
        send_sem=send_sem,
        recv_sem=recv_sem,
        device_id={"vec": sibling},
        device_id_type=mesh_ids,
    )
    copy.start()
    out_ref[core] = x_ref[...]
    copy.wait()
    out_ref[sibling] = recv_ref[...]


def gathered_over_vec(block):
    halves = pl.pallas_call(
        swap_halves,
        out_shape=jax.ShapeDtypeStruct((2, *block.shape), block.dtype),
        in_specs=[pl.BlockSpec(memory_space=pltpu.VMEM)],
        out_specs=pl.BlockSpec(memory_space=pltpu.VMEM),
        scratch_shapes=[
            pltpu.VMEM(block.shape, block.dtype),
            pltpu.SemaphoreType.DMA(()),
            pltpu.SemaphoreType.DMA(()),
        ],
        compiler_params=pltpu.CompilerParams(collective_id=2, has_side_effects=True),
    )(block)
    return jnp.concatenate([halves[0], halves[1]], axis=1)


def tile_products(rows_ref, cols_ref, used_ref, tile_ref, x_ref, out_ref):
    slot = pl.program_id(0)

    @pl.when(slot == 0)
    def _():
        out_ref[...] = jnp.zeros_like(out_ref)

    @pl.when(slot < used_ref[0])
    def _():
        row = rows_ref[slot]
        col = cols_ref[slot]
        tile = tile_ref[0]
        weight = jnp.where(row == col, jnp.float32(0.5), jnp.float32(1.0))
        direct = jnp.dot(tile, x_ref[col], preferred_element_type=jnp.float32)
        out_ref[row] += direct * weight
        mirror = lax.dot_general(
            tile, x_ref[row], (((0,), (0,)), ((), ())), preferred_element_type=jnp.float32
        )
        out_ref[col] += mirror * weight


def hessian_window(window_x, blocks, rows_local, cols_local, used):
    slots, tile_size, _ = blocks.shape
    window_tiles, _, col_width = window_x.shape

    def tile_at(slot, rows, cols, used_ref):
        return (jnp.maximum(jnp.minimum(slot, used_ref[0] - 1), 0), 0, 0)

    def whole(slot, rows, cols, used_ref):
        return (0, 0, 0)

    grid_spec = pltpu.PrefetchScalarGridSpec(
        num_scalar_prefetch=3,
        grid=(slots,),
        in_specs=[
            pl.BlockSpec((1, tile_size, tile_size), tile_at),
            pl.BlockSpec((window_tiles, tile_size, col_width), whole),
        ],
        out_specs=pl.BlockSpec((window_tiles, tile_size, col_width), whole),
    )
    flops = 4 * slots * tile_size * tile_size * col_width
    return pl.pallas_call(
        tile_products,
        grid_spec=grid_spec,
        out_shape=jax.ShapeDtypeStruct((window_tiles, tile_size, col_width), jnp.float32),
        compiler_params=pltpu.CompilerParams(dimension_semantics=("arbitrary",)),
        cost_estimate=pl.CostEstimate(
            flops=flops,
            bytes_accessed=blocks.size * 2 + window_x.size * 2 + window_tiles * tile_size * col_width * 4,
            transcendentals=0,
        ),
    )(rows_local, cols_local, used, blocks, window_x)


def accumulate(window_x, totals, block_tiles, row_ids, col_ids, used_slots, window_start):
    group_total = (used_slots + 7) // 8

    def one_turn(group_index, partial_value):
        first_slot = group_index * 8
        chosen = lax.dynamic_slice_in_dim(block_tiles, first_slot, 8, 0)
        rows_here = lax.dynamic_slice_in_dim(row_ids, first_slot, 8, 0) - window_start
        cols_here = lax.dynamic_slice_in_dim(col_ids, first_slot, 8, 0) - window_start
        alive_mask = (first_slot + jnp.arange(8, dtype=jnp.int32) < used_slots).astype(jnp.float32)
        weight = (jnp.where(rows_here == cols_here, 0.5, 1.0).astype(jnp.float32) * alive_mask)[
            :, None, None
        ]
        direct = (
            jnp.einsum(
                "sab,sbk->sak", chosen, window_x[cols_here], preferred_element_type=jnp.float32
            )
            * weight
        )
        mirror = (
            jnp.einsum(
                "sba,sbk->sak", chosen, window_x[rows_here], preferred_element_type=jnp.float32
            )
            * weight
        )
        return partial_value.at[rows_here].add(direct).at[cols_here].add(mirror)

    return lax.fori_loop(0, group_total, one_turn, totals)


def shards(vectors, blocks, block_row, block_col, block_count):
    dev_rows, col_width = vectors.shape
    tile_size = blocks.shape[1]
    total_rows = dev_rows * lax.axis_size("patch")
    position = lax.axis_index("patch")
    parity = position % 2
    window_start = 2 * (position - 6 - parity)
    column_start = lax.axis_index("vec") * col_width
    used_slots = block_count[0]
    current = vectors
    residual = vectors
    for iteration in range(STEPS):
        rounded = current.astype(jnp.bfloat16)
        pieces = {0: rounded}
        for offset in (7, 6, 5, 4, 3, 2, 1, -1):
            pieces[offset] = shifted(rounded, "patch", offset)
        lower_side = jnp.concatenate([pieces[6 - segment] for segment in range(8)], axis=0)
        upper_side = jnp.concatenate([pieces[7 - segment] for segment in range(8)], axis=0)
        window_x = jnp.where(parity == 0, lower_side, upper_side).reshape(16, tile_size, col_width)
        totals = hessian_window(
            window_x, blocks, block_row - window_start, block_col - window_start, block_count
        )
        segments = totals.reshape(8, dev_rows, col_width)
        zero_rows = jnp.zeros((dev_rows, col_width), jnp.float32)
        applied = jnp.where(parity == 0, segments[6], segments[7])
        for offset in (1, -1, -2, -3, -4, -5, -6, -7):
            lower_seg = segments[offset + 6] if 0 <= offset + 6 <= 7 else zero_rows
            upper_seg = segments[offset + 7] if 0 <= offset + 7 <= 7 else zero_rows
            outgoing = jnp.where(parity == 0, lower_seg, upper_seg)
            applied = applied + shifted(outgoing, "patch", offset)
        current_all = gathered_over_vec(current)
        rayleigh = summed_over_patch(
            jnp.dot(
                current_all.T, applied, precision=exact_mode, preferred_element_type=jnp.float32
            )
            / total_rows,
            0,
        )
        residual = applied - jnp.dot(
            current_all, rayleigh, precision=exact_mode, preferred_element_type=jnp.float32
        )
        update = current - step_rate * residual
        update_all = gathered_over_vec(update)
        gram_matrix = gathered_over_vec(
            summed_over_patch(
                jnp.dot(update_all.T, update, precision=exact_mode, preferred_element_type=jnp.float32)
                / total_rows,
                0,
            )
        )
        factor = jnp.linalg.cholesky(gram_matrix)
        solved = lax.linalg.triangular_solve(
            factor, update_all, left_side=False, lower=True, transpose_a=True
        )
        current = lax.dynamic_slice_in_dim(solved, column_start, col_width, 1)
    return (current, residual)


def solution(mesh):
    in_specs = (P("patch", "vec"), P("patch", None, None), P("patch"), P("patch"), P("patch"))
    out_specs = (P("patch", "vec"), P("patch", "vec"))
    return jax.shard_map(shards, mesh=mesh, in_specs=in_specs, out_specs=out_specs, check_vma=False)
```
